512 devices in a mesh: span: 64 (over z, x), width: 8 (over y, core).
Axes of the slice: x: 4, y: 4, z: 16, core: 2. Of those that a mesh axis runs over, the one named last changes fastest.
Arguments:
- right_side: float32 [32, 512, 4096], P(None, 'span', 'width'), may hold values from -6 to 6
- diffusivity: float32 [32, 512, 4096], P(None, 'span', 'width'), may hold values from 0.2 to 5
- reaction: float32 [32, 512, 4096], P(None, 'span', 'width'), may hold values from 0.01 to 0.2
Outputs:
- correction: float32 [32, 512, 4096], P(None, 'span', 'width')
The draws below stay inside these ranges and needn't reach their ends.
All inputs are finite; a program needn't handle non-finite values.
Results may differ from the reference program's by a relative error of at most 0.0003.
Values sent between devices are 32-bit elements; how exact they have to be, the bound alone decides.
A program may use at most 128 MiB of HBM per device.

```python
import math
import jax
import jax.numpy as jnp

NZ = 32
LEVELS = 6
COARSE_SWEEPS = 3
NX = 512
NY = 4096


def steps_of(rng, extent, cuts, least, largest):
    def one(dim, parts):
        steps = jax.random.uniform(jax.random.fold_in(jax.random.fold_in(rng, 6), dim), (parts,), jnp.float32, least / len(cuts), largest / len(cuts))
        return jnp.repeat(jnp.exp(steps), extent[dim] // parts).reshape((-1,) + (1,) * (len(extent) - dim - 1))

    factor_of = one(*cuts[0])
    for cut in cuts[1:]:
        factor_of = factor_of * one(*cut)
    return factor_of


def normal_values(own_key, extent, spread, reach, shards=(), kind=jnp.bfloat16):
    array = spread * jax.random.normal(own_key, extent, jnp.float32)
    if shards:
        array = array * steps_of(own_key, extent, shards, -0.22, 0.18)
    return jnp.clip(array, -reach, reach).astype(kind)


def setup_inputs(seed: int = 0) -> dict:
    arg_keys = jax.random.split(jax.random.key(seed), 4)
    right_side = normal_values(arg_keys[0], (NZ, NX, NY), 1.0, 6.0, ((1, 64), (2, 8)), jnp.float32)
    diffusivity = jnp.clip(jnp.exp(math.log(5.0) - 3.218876 * jax.random.uniform(arg_keys[1], (NZ, NX, NY), jnp.float32) ** steps_of(arg_keys[1], (NZ, NX, NY), ((1, 64), (2, 8)), -0.2, 0.2)), 0.2, 5.0)
    reaction = jnp.clip(jnp.exp(math.log(0.2) - 2.9957323 * jax.random.uniform(arg_keys[2], (NZ, NX, NY), jnp.float32) ** steps_of(arg_keys[2], (NZ, NX, NY), ((1, 64), (2, 8)), -0.2, 0.2)), 0.01, 0.2)
    return {"right_side": right_side, "diffusivity": diffusivity, "reaction": reaction}


relax_weight = 0.8


def harmonic(first, second):
    return 2.0 * first * second / (first + second)


def face_terms(diffusivity, reaction, grid_level):
    padded = jnp.pad(diffusivity, ((1, 1), (1, 1), (1, 1)))
    face_scale = 0.25 ** grid_level
    west = face_scale * harmonic(diffusivity, padded[1:-1, :-2, 1:-1])
    east = face_scale * harmonic(diffusivity, padded[1:-1, 2:, 1:-1])
    south = face_scale * harmonic(diffusivity, padded[1:-1, 1:-1, :-2])
    north = face_scale * harmonic(diffusivity, padded[1:-1, 1:-1, 2:])
    upward = face_scale * harmonic(diffusivity, padded[:-2, 1:-1, 1:-1])
    downward = face_scale * harmonic(diffusivity, padded[2:, 1:-1, 1:-1])
    diagonal = west + east + south + north + upward + downward + face_scale * reaction
    return (west, east, south, north, upward, downward, diagonal)


def operate(field, coeffs):
    padded = jnp.pad(field, ((1, 1), (1, 1), (1, 1)))
    beside = coeffs[0] * padded[1:-1, :-2, 1:-1] + coeffs[1] * padded[1:-1, 2:, 1:-1]
    beside = beside + coeffs[2] * padded[1:-1, 1:-1, :-2] + coeffs[3] * padded[1:-1, 1:-1, 2:]
    beside = beside + coeffs[4] * padded[:-2, 1:-1, 1:-1] + coeffs[5] * padded[2:, 1:-1, 1:-1]
    return coeffs[6] * field - beside


def restrict(field):
    depth, first, second = field.shape
    return jnp.mean(field.reshape(depth, first // 2, 2, second // 2, 2), axis=(2, 4))


def prolong(field):
    return jnp.repeat(jnp.repeat(field, 2, axis=1), 2, axis=2)


def reference(right_side, diffusivity, reaction):
    source = right_side
    conduct = diffusivity
    binding = reaction
    saved = []
    for grid_level in range(LEVELS - 1):
        coeffs = face_terms(conduct, binding, grid_level)
        smooth_one = relax_weight * source / coeffs[6]
        defect = source - operate(smooth_one, coeffs)
        saved.append((source, smooth_one, conduct, binding))
        source = restrict(defect)
        conduct = restrict(conduct)
        binding = restrict(binding)
    coeffs = face_terms(conduct, binding, LEVELS - 1)
    iterate = relax_weight * source / coeffs[6]
    for sweep_index in range(COARSE_SWEEPS - 1):
        iterate = iterate + relax_weight * (source - operate(iterate, coeffs)) / coeffs[6]
    for grid_level in range(LEVELS - 2, -1, -1):
        source, smooth_one, conduct, binding = saved[grid_level]
        coeffs = face_terms(conduct, binding, grid_level)
        lifted = smooth_one + prolong(iterate)
        iterate = lifted + relax_weight * (source - operate(lifted, coeffs)) / coeffs[6]
    return iterate
```

```python
import jax
import jax.numpy as jnp
from jax import lax
from jax.experimental import pallas as pl
from jax.experimental.pallas import tpu as pltpu
from jax.sharding import PartitionSpec as P


MESH = pl.DeviceIdType.MESH
F32 = jnp.float32
WEIGHT = 0.8
NZ = 32
LANES = 128
SPAN = 64
WIDTH = 8
ROWS = (12, 8, 6, 12, 6, 9)
TILES = (6, 3, 2, 1, 1, 1)
GRID_ROWS = (512, 256, 128, 64, 32, 16)
N_SEMS = 80


class Level:
    def __init__(self, index, refs, base, width_at):
        self.index, self.base, self.width_at = index, base, width_at
        self.tiles = TILES[index]
        self.conduct, self.binding, self.source, self.smooth, self.fx, self.fy, self.fz, self.weight, self.work = refs
        self.scale = 0.25**index

    def cut(self, row):
        at = lax.rem(self.base + (row + 1 + GRID_ROWS[self.index]), GRID_ROWS[self.index])
        return jnp.where(at == 0, 0.0, 2.0 * self.scale).astype(F32)

    def y_factor(self, tile):
        halo, own = LANES >> self.index, 512 >> self.index
        low, high = halo - 1, halo + own - 1
        full = jnp.full((NZ, LANES), 2.0 * self.scale, F32)
        lane = lax.broadcasted_iota(jnp.int32, (NZ, LANES), 1)
        for place, edge in ((low, 0), (high, WIDTH - 1)):
            if place // LANES == tile:
                spot = jnp.where(self.width_at == edge, place % LANES, -1)
                full = jnp.where(lane == spot, 0.0, full)
        return full

    def z_factor(self):
        depth = lax.broadcasted_iota(jnp.int32, (NZ, LANES), 0)
        return jnp.where(depth == NZ - 1, 0.0, 2.0 * self.scale)


def tile_of(ref, row, tile):
    return ref[row, :, pl.ds(tile * LANES, LANES)]


def put(ref, row, tile, value):
    ref[row, :, pl.ds(tile * LANES, LANES)] = value


def for_rows(first, last, body, unrolled):
    if unrolled:
        for row in range(first, last):
            body(row)
    else:
        lax.fori_loop(first, last, lambda row, carry: (body(row), carry)[1], 0)


def lane_above(tiles, tile):
    here = tiles[tile]
    after = tiles[min(tile + 1, len(tiles) - 1)]
    lane = lax.broadcasted_iota(jnp.int32, here.shape, 1)
    return pltpu.roll(jnp.where(lane == 0, after, here), LANES - 1, 1)


def lane_below(tiles, tile):
    here = tiles[tile]
    before = tiles[max(tile - 1, 0)]
    lane = lax.broadcasted_iota(jnp.int32, here.shape, 1)
    return pltpu.roll(jnp.where(lane == LANES - 1, before, here), 1, 1)


def depth_above(value):
    return pltpu.roll(value, NZ - 1, 0)


def depth_below(value):
    return pltpu.roll(value, 1, 0)


def mean_face(factor, first, second):
    return factor * (first * second) / (first + second)


def faces(level, first, last, unrolled):
    def x_faces(row):
        factor = level.cut(row)
        for tile in range(level.tiles):
            put(level.fx, row, tile, mean_face(factor, tile_of(level.conduct, row, tile), tile_of(level.conduct, row + 1, tile)))

    def one(row):
        x_faces(row)
        cells = [tile_of(level.conduct, row, tile) for tile in range(level.tiles)]
        beside = [mean_face(level.y_factor(tile), cells[tile], lane_above(cells, tile)) for tile in range(level.tiles)]
        for tile in range(level.tiles):
            deep = mean_face(level.z_factor(), cells[tile], depth_above(cells[tile]))
            diagonal = tile_of(level.fx, row - 1, tile) + tile_of(level.fx, row, tile)
            diagonal = diagonal + lane_below(beside, tile) + beside[tile]
            diagonal = diagonal + depth_below(deep) + deep + level.scale * tile_of(level.binding, row, tile)
            put(level.fy, row, tile, beside[tile])
            put(level.fz, row, tile, deep)
            put(level.weight, row, tile, WEIGHT / diagonal)

    x_faces(first - 1)
    for_rows(first, last, one, unrolled)


def smooth(level, first, last, unrolled):
    def one(row):
        for tile in range(level.tiles):
            put(level.smooth, row, tile, tile_of(level.weight, row, tile) * tile_of(level.source, row, tile))

    for_rows(first, last, one, unrolled)


def residual(level, field, row):
    cells = [tile_of(field, row, tile) for tile in range(level.tiles)]
    along = [tile_of(level.fy, row, tile) * (lane_above(cells, tile) - cells[tile]) for tile in range(level.tiles)]
    out = []
    for tile in range(level.tiles):
        here = cells[tile]
        deep = tile_of(level.fz, row, tile) * (depth_above(here) - here)
        value = tile_of(level.source, row, tile) - level.scale * tile_of(level.binding, row, tile) * here
        value = value + tile_of(level.fx, row, tile) * (tile_of(field, row + 1, tile) - here)
        value = value - tile_of(level.fx, row - 1, tile) * (here - tile_of(field, row - 1, tile))
        value = value + (along[tile] - lane_below(along, tile)) + (deep - depth_below(deep))
        out.append(value)
    return out


def relax(level, field, first, last, store, unrolled):
    def one(row):
        rest = residual(level, field, row)
        for tile in range(level.tiles):
            store(row, tile, tile_of(field, row, tile) + tile_of(level.weight, row, tile) * rest[tile])

    for_rows(first, last, one, unrolled)


def exact_dot(value, selector):
    high = value.astype(jnp.bfloat16)
    left = value - high.astype(F32)
    middle = left.astype(jnp.bfloat16)
    low = (left - middle.astype(F32)).astype(jnp.bfloat16)
    total = jnp.dot(low, selector, preferred_element_type=F32) + jnp.dot(middle, selector, preferred_element_type=F32)
    return total + jnp.dot(high, selector, preferred_element_type=F32)


def coarsen(tiles_in, coarse_tiles, select):
    out = []
    for tile in range(coarse_tiles):
        if 2 * tile + 1 < len(tiles_in):
            pair = jnp.concatenate([tiles_in[2 * tile], tiles_in[2 * tile + 1]], axis=1)
            out.append(exact_dot(pair, select[0]))
        else:
            out.append(exact_dot(tiles_in[2 * tile], select[1]))
    return out


def kernel(right_ref, conduct_ref, binding_ref, out_ref, *scratch):
    levels_refs, (raw, raw_out, local_sem, coarse_send, coarse_recv) = scratch[:-5], scratch[-5:]
    loads = []
    for i, ref in enumerate((conduct_ref, right_ref, binding_ref)):
        for t in range(4):
            loads.append(pltpu.make_async_copy(ref.at[:, pl.ds(t * LANES, LANES)], raw.at[i, t], local_sem.at[4 * i + t]))
            loads[-1].start()
    span_at, width_at = lax.axis_index("span"), lax.axis_index("width")
    plane, across = span_at // 4, lax.rem(span_at, 4)
    d0, sb0, db1, s1, db2, s2, db3, s3, db5, s5 = levels_refs[:10]
    rest = list(levels_refs[10:])

    def take():
        return rest.pop(0)

    base = (8 * span_at - 2, 4 * span_at - 2, 2 * span_at - 2, 4 * plane - 4, 2 * plane - 2, plane - 4)
    d4, b4, s4 = take(), take(), take()
    own = [
        (d0, sb0.at[1], sb0.at[0]),
        (db1.at[0], db1.at[1], s1),
        (db2.at[0], db2.at[1], s2),
        (db3.at[0], db3.at[1], s3),
        (d4, b4, s4),
        (db5.at[0], db5.at[1], s5),
    ]
    levels = [Level(i, own[i] + tuple(take() for _ in range(6)), base[i], width_at) for i in range(6)]
    sums = take()
    lifts = take()
    iterates = [take() for _ in range(6)]

    def device(across_span, across_width=0):
        return (lax.rem(span_at + (across_span + SPAN), SPAN), lax.rem(width_at + (across_width + WIDTH), WIDTH))

    ring = [(dz, dx) for dz in (0, 1, -1) for dx in range(4) if (dz, dx) != (0, 0)]

    def ring_device(dz, dx):
        to = lax.rem(across + dx, 4)
        return (lax.rem(4 * plane + (4 * dz + SPAN) + to, SPAN), width_at)

    around = [(1, 0), (-1, 0), (0, 1), (0, -1), (1, 1), (1, -1), (-1, 1), (-1, -1)]
    far = [(dz, 0) for dz in (2, -2, 3, -3, 4, -4)]

    barrier = pltpu.get_barrier_semaphore()
    partners = [ring_device(dz, dx) for dz, dx in ring] + [device(4 * dz) for dz, _ in far]
    partners += [device(a, b) for a, b in around if b != 0]
    for partner in partners:
        pl.semaphore_signal(barrier, inc=1, device_id=partner, device_id_type=MESH)

    lane = lax.broadcasted_iota(jnp.int32, (2 * LANES, LANES), 0) // 2
    column = lax.broadcasted_iota(jnp.int32, (2 * LANES, LANES), 1)
    pair_select = jnp.where(lane == column, 0.25, 0.0).astype(jnp.bfloat16)
    lane = lax.broadcasted_iota(jnp.int32, (LANES, LANES), 0) // 2
    column = lax.broadcasted_iota(jnp.int32, (LANES, LANES), 1)
    twice_select = jnp.where(lane == lax.rem(column, LANES // 2), 0.25, 0.0).astype(jnp.bfloat16)
    select = (pair_select, twice_select)
    lane = lax.broadcasted_iota(jnp.int32, (LANES, LANES), 0)
    column = lax.broadcasted_iota(jnp.int32, (LANES, LANES), 1) // 2
    spread = tuple(jnp.where(lane == column + half * (LANES // 2), 1.0, 0.0).astype(jnp.bfloat16) for half in (0, 1))

    for i, ref in enumerate((d0, sb0.at[0], sb0.at[1])):
        for t in range(4):
            loads[4 * i + t].wait()
            for row in range(8):
                put(ref, 2 + row, 1 + t, raw[i, t, pl.ds(row, NZ, stride=8), :])

    pl.semaphore_wait(barrier, len(partners))

    copies = []

    def send(source, target, to):
        at = len(copies)
        copy = pltpu.make_async_remote_copy(
            src_ref=source, dst_ref=target, send_sem=coarse_send.at[at], recv_sem=coarse_recv.at[at], device_id=to, device_id_type=MESH
        )
        copy.start()
        copies.append(copy)
        return copy

    def arrive(group):
        for copy in group:
            copy.wait_recv()

    first = []
    for a, b in around:
        lanes_from, lanes_to = {0: (pl.ds(LANES, 4 * LANES),) * 2, 1: (pl.ds(4 * LANES, LANES), pl.ds(0, LANES)), -1: (pl.ds(LANES, LANES), pl.ds(5 * LANES, LANES))}[b]
        from_2, to_2 = {0: (pl.ds(2, 8),) * 2, 1: (pl.ds(8, 2), pl.ds(0, 2)), -1: (pl.ds(2, 2), pl.ds(10, 2))}[a]
        from_1, to_1 = {0: (pl.ds(2, 8),) * 2, 1: (pl.ds(9, 1), pl.ds(1, 1)), -1: (pl.ds(2, 1), pl.ds(10, 1))}[a]
        first.append(send(d0.at[from_2, :, lanes_from], d0.at[to_2, :, lanes_to], device(a, b)))
        first.append(send(sb0.at[:, from_1, :, lanes_from], sb0.at[:, to_1, :, lanes_to], device(a, b)))
    arrive(first)

    def coarse_fields(fine, coarse, n_rows, fine_row, coarse_row, fill_rows=None):
        for pick_fine, pick_coarse in ((fine.conduct, coarse.conduct), (fine.binding, coarse.binding)):
            tiles = [
                jnp.concatenate([tile_of(pick_fine, fine_row + 2 * i, t) + tile_of(pick_fine, fine_row + 2 * i + 1, t) for i in range(n_rows)], axis=0)
                for t in range(fine.tiles)
            ]
            for t, value in enumerate(coarsen(tiles, coarse.tiles, select)):
                for i in range(n_rows):
                    put(pick_coarse, coarse_row + i, t, value[i * NZ : (i + 1) * NZ])

    def coarse_source(fine, coarse, n_rows, fine_row, coarse_row, unrolled):
        def one(i):
            low = residual(fine, fine.smooth, fine_row + 2 * i)
            high = residual(fine, fine.smooth, fine_row + 2 * i + 1)
            for t in range(fine.tiles):
                put(sums, i, t, low[t] + high[t])

        for_rows(0, n_rows, one, unrolled)
        tiles = [jnp.concatenate([tile_of(sums, i, t) for i in range(n_rows)], axis=0) for t in range(fine.tiles)]
        for t, value in enumerate(coarsen(tiles, coarse.tiles, select)):
            for i in range(n_rows):
                put(coarse.source, coarse_row + i, t, value[i * NZ : (i + 1) * NZ])

    l0, l1, l2, l3, l4, l5 = levels

    coarse_fields(l0, l1, 4, 2, 2)
    fields_1 = []
    for to, d_from, d_to, b_from, b_to in ((1, 4, 0, 5, 1), (-1, 2, 6, 2, 6)):
        fields_1.append(send(db1.at[0, pl.ds(d_from, 2)], db1.at[0, pl.ds(d_to, 2)], device(to)))
        fields_1.append(send(db1.at[1, pl.ds(b_from, 1)], db1.at[1, pl.ds(b_to, 1)], device(to)))
    coarse_fields(l1, l2, 2, 2, 2)
    fields_2 = []
    for to, d_from, d_to, b_from, b_to in ((1, 2, 0, 3, 1), (-1, 2, 4, 2, 4)):
        fields_2.append(send(db2.at[0, pl.ds(d_from, 2)], db2.at[0, pl.ds(d_to, 2)], device(to)))
        fields_2.append(send(db2.at[1, pl.ds(b_from, 1)], db2.at[1, pl.ds(b_to, 1)], device(to)))
    mine = 4 + across
    coarse_fields(l2, l3, 1, 2, mine)
    fields_3 = [
        send(db3.at[:, pl.ds(mine, 1)], db3.at[:, pl.ds(4 * (1 - dz) + across, 1)], ring_device(dz, dx)) for dz, dx in ring
    ]

    faces(l0, 1, 11, False)
    smooth(l0, 1, 11, False)
    coarse_source(l0, l1, 4, 2, 2, False)

    sources_1 = [send(s1.at[pl.ds(5, 1)], s1.at[pl.ds(1, 1)], device(1)), send(s1.at[pl.ds(2, 1)], s1.at[pl.ds(6, 1)], device(-1))]
    arrive(fields_1)
    faces(l1, 1, 7, False)
    arrive(fields_3)
    coarse_fields(l3, l4, 6, 0, 0)
    coarse_fields(l4, l5, 1, 2, 4)
    fields_5 = [
        send(db5.at[:, pl.ds(4, 1)], db5.at[:, pl.ds(4 - dz, 1)], device(4 * dz)) for dz in (1, -1, 2, -2, 3, -3, 4, -4)
    ]
    arrive(sources_1)
    smooth(l1, 1, 7, False)
    coarse_source(l1, l2, 2, 2, 2, False)

    sources_2 = [send(s2.at[pl.ds(3, 1)], s2.at[pl.ds(1, 1)], device(1)), send(s2.at[pl.ds(2, 1)], s2.at[pl.ds(4, 1)], device(-1))]
    smooths_1 = [send(l1.smooth.at[pl.ds(4, 1)], l1.smooth.at[pl.ds(0, 1)], device(1)), send(l1.smooth.at[pl.ds(3, 1)], l1.smooth.at[pl.ds(7, 1)], device(-1))]
    arrive(fields_2)
    faces(l2, 1, 5, True)
    arrive(sources_2)
    smooth(l2, 1, 5, True)
    coarse_source(l2, l3, 1, 2, mine, True)

    sources_3 = [
        send(s3.at[pl.ds(mine, 1)], s3.at[pl.ds(4 * (1 - dz) + across, 1)], ring_device(dz, dx)) for dz, dx in ring
    ]
    smooths_2 = [send(l2.smooth.at[pl.ds(2, 1)], l2.smooth.at[pl.ds(0, 1)], device(1)), send(l2.smooth.at[pl.ds(3, 1)], l2.smooth.at[pl.ds(5, 1)], device(-1))]
    faces(l3, 1, 11, False)
    faces(l4, 1, 5, True)
    arrive(sources_3)
    smooth(l3, 1, 11, True)
    coarse_source(l3, l4, 4, 2, 1, False)
    smooth(l4, 1, 5, True)
    coarse_source(l4, l5, 1, 2, 4, True)

    sources_5 = [send(s5.at[pl.ds(4, 1)], s5.at[pl.ds(4 - dz, 1)], device(4 * dz)) for dz in (1, -1, 2, -2, 3, -3)]
    smooths_4 = [send(l4.smooth.at[pl.ds(2, 1)], l4.smooth.at[pl.ds(0, 1)], device(-4 * -1)), send(l4.smooth.at[pl.ds(3, 1)], l4.smooth.at[pl.ds(5, 1)], device(-4))]
    arrive(fields_5)
    faces(l5, 1, 8, True)
    arrive(sources_5)

    smooth(l5, 1, 8, True)

    def into(ref):
        return lambda row, tile, value: put(ref, row, tile, value)

    relax(l5, l5.smooth, 2, 7, into(l5.work), True)
    relax(l5, l5.work, 3, 6, into(iterates[5]), True)

    def lift(fine, coarse_ref, coarse_rows, coarse_tiles, first_row, last_row, coarse_of):
        values = [jnp.concatenate([tile_of(coarse_ref, c, t) for c in coarse_rows], axis=0) for t in range(coarse_tiles)]
        for t in range(fine.tiles):
            spread_out = exact_dot(values[t // 2], spread[t % 2])
            for row in range(first_row, last_row):
                at = coarse_of(row)
                put(lifts, row, t, tile_of(fine.smooth, row, t) + spread_out[at * NZ : (at + 1) * NZ])

    arrive(smooths_4)
    lift(l4, iterates[5], range(3, 6), 1, 0, 6, lambda row: row // 2)
    relax(l4, lifts, 1, 5, into(iterates[4]), True)
    lift(l3, iterates[4], range(1, 5), 1, 2, 10, lambda row: row // 2 - 1)
    relax(l3, lifts, 3, 9, into(iterates[3]), True)
    arrive(smooths_2)
    lift(l2, iterates[3], [across + 3 + i for i in range(3)], 1, 0, 6, lambda row: row // 2)
    relax(l2, lifts, 1, 5, into(iterates[2]), True)
    arrive(smooths_1)
    lift(l1, iterates[2], range(1, 5), 2, 0, 8, lambda row: row // 2)
    relax(l1, lifts, 1, 7, into(iterates[1]), False)
    lift(l0, iterates[1], range(1, 7), 3, 1, 11, lambda row: (row - 2) // 2 + 1)

    def finish(row, tile, value):
        if 1 <= tile <= 4:
            raw_out[tile - 1, pl.ds(row - 2, NZ, stride=8), :] = value

    relax(l0, lifts, 2, 10, finish, False)
    stores = []
    for t in range(4):
        stores.append(pltpu.make_async_copy(raw_out.at[t], out_ref.at[:, pl.ds(t * LANES, LANES)], local_sem.at[t]))
        stores[-1].start()
    for copy in stores:
        copy.wait()

    for copy in copies:
        copy.wait_send()


def shapes():
    def rows(level, *lead):
        return pltpu.VMEM((*lead, ROWS[level], NZ, TILES[level] * LANES), F32)

    first = [rows(0), rows(0, 2), rows(1, 2), rows(1), rows(2, 2), rows(2), rows(3, 2), rows(3), rows(5, 2), rows(5)]
    first += [rows(4), rows(4), rows(4)]
    for level in range(6):
        first += [rows(level) for _ in range(6)]
    first += [pltpu.VMEM((4, NZ, TILES[0] * LANES), F32), pltpu.VMEM((12, NZ, TILES[0] * LANES), F32)]
    first += [rows(level) for level in range(6)]
    first += [pltpu.VMEM((3, 4, NZ * 8, LANES), F32), pltpu.VMEM((4, NZ * 8, LANES), F32), pltpu.SemaphoreType.DMA((12,))]
    return first + [pltpu.SemaphoreType.DMA((N_SEMS,)), pltpu.SemaphoreType.DMA((N_SEMS,))]


def on_device(right_side, diffusivity, reaction):
    flat = [field.reshape(NZ * 8, 512) for field in (right_side, diffusivity, reaction)]
    out = pl.pallas_call(
        kernel,
        out_shape=jax.ShapeDtypeStruct((NZ * 8, 512), F32),
        in_specs=[pl.BlockSpec(memory_space=pl.ANY)] * 3,
        out_specs=pl.BlockSpec(memory_space=pl.ANY),
        scratch_shapes=shapes(),
        compiler_params=pltpu.CompilerParams(collective_id=0, has_side_effects=True, vmem_limit_bytes=48 << 20),
    )(*flat)
    return out.reshape(NZ, 8, 512)


def solution(mesh):
    specs = P(None, "span", "width")
    return jax.shard_map(on_device, mesh=mesh, in_specs=(specs,) * 3, out_specs=specs, check_vma=False)
```

```python
import jax
import jax.numpy as jnp
from jax import lax
from jax.experimental import pallas as pl
from jax.experimental.pallas import tpu as pltpu
from jax.sharding import PartitionSpec as P


MESH = pl.DeviceIdType.MESH
F32 = jnp.float32
WEIGHT = 0.8
NZ = 32
LANES = 128
SPAN = 64
WIDTH = 8
ROWS = (12, 8, 6, 12, 6, 9)
TILES = (6, 3, 2, 1, 1, 1)
GRID_ROWS = (512, 256, 128, 64, 32, 16)
N_SEMS = 96
VMEM_BYTES = 62 << 20


class Level:
    def __init__(self, index, refs, base, width_at):
        self.index, self.base, self.width_at = index, base, width_at
        self.tiles = TILES[index]
        self.conduct, self.binding, self.source, self.smooth, self.fx, self.fy, self.fz, self.weight, self.work = refs
        self.scale = 0.25**index

    def cut(self, row):
        at = lax.rem(self.base + (row + 1 + GRID_ROWS[self.index]), GRID_ROWS[self.index])
        return jnp.where(at == 0, 0.0, 2.0 * self.scale).astype(F32)

    def y_factor(self, tile):
        halo, own = LANES >> self.index, 512 >> self.index
        low, high = halo - 1, halo + own - 1
        full = jnp.full((NZ, LANES), 2.0 * self.scale, F32)
        lane = lax.broadcasted_iota(jnp.int32, (NZ, LANES), 1)
        for place, edge in ((low, 0), (high, WIDTH - 1)):
            if place // LANES == tile:
                spot = jnp.where(self.width_at == edge, place % LANES, -1)
                full = jnp.where(lane == spot, 0.0, full)
        return full

    def y_factors(self):
        return [self.y_factor(tile) for tile in range(self.tiles)]

    def z_factor(self):
        depth = lax.broadcasted_iota(jnp.int32, (NZ, LANES), 0)
        return jnp.where(depth == NZ - 1, 0.0, 2.0 * self.scale)


def tile_of(ref, row, tile):
    return ref[row, :, pl.ds(tile * LANES, LANES)]


def put(ref, row, tile, value):
    ref[row, :, pl.ds(tile * LANES, LANES)] = value


def for_rows(first, last, body, unrolled):
    if unrolled:
        for row in range(first, last):
            body(row)
    else:
        lax.fori_loop(first, last, lambda row, carry: (body(row), carry)[1], 0)


def lane_above(tiles, tile):
    here = tiles[tile]
    after = tiles[min(tile + 1, len(tiles) - 1)]
    lane = lax.broadcasted_iota(jnp.int32, here.shape, 1)
    return pltpu.roll(jnp.where(lane == 0, after, here), LANES - 1, 1)


def lane_below(tiles, tile):
    here = tiles[tile]
    before = tiles[max(tile - 1, 0)]
    lane = lax.broadcasted_iota(jnp.int32, here.shape, 1)
    return pltpu.roll(jnp.where(lane == LANES - 1, before, here), 1, 1)


def depth_above(value):
    return pltpu.roll(value, NZ - 1, 0)


def depth_below(value):
    return pltpu.roll(value, 1, 0)


def mean_face(factor, first, second):
    return factor * (first * second) / (first + second)


def face_x(level, row, tiles):
    factor = level.cut(row)
    for tile in tiles:
        put(level.fx, row, tile, mean_face(factor, tile_of(level.conduct, row, tile), tile_of(level.conduct, row + 1, tile)))


def face_y(level, row, tiles, factors):
    for tile in tiles:
        near = {t: tile_of(level.conduct, row, t) for t in {tile, min(tile + 1, level.tiles - 1)}}
        after = near[min(tile + 1, level.tiles - 1)]
        put(level.fy, row, tile, mean_face(factors[tile], near[tile], lane_above((near[tile], after), 0)))


def face_z(level, row, tiles, factor):
    for tile in tiles:
        here = tile_of(level.conduct, row, tile)
        put(level.fz, row, tile, mean_face(factor, here, depth_above(here)))


def weigh(level, row, tiles):
    for tile in tiles:
        beside, deep = tile_of(level.fy, row, tile), tile_of(level.fz, row, tile)
        before = tile_of(level.fy, row, max(tile - 1, 0))
        diagonal = tile_of(level.fx, row - 1, tile) + tile_of(level.fx, row, tile)
        diagonal = diagonal + lane_below((before, beside), 1) + beside
        diagonal = diagonal + depth_below(deep) + deep + level.scale * tile_of(level.binding, row, tile)
        put(level.weight, row, tile, WEIGHT / diagonal)


def faces(level, first, last, unrolled):
    tiles = range(level.tiles)
    factors, deep_factor = level.y_factors(), level.z_factor()

    def one(row):
        face_x(level, row, tiles)
        face_y(level, row, tiles, factors)
        face_z(level, row, tiles, deep_factor)
        weigh(level, row, tiles)

    face_x(level, first - 1, tiles)
    for_rows(first, last, one, unrolled)


def smooth(level, first, last, unrolled):
    def one(row):
        for tile in range(level.tiles):
            put(level.smooth, row, tile, tile_of(level.weight, row, tile) * tile_of(level.source, row, tile))

    for_rows(first, last, one, unrolled)


def residual(level, field, row):
    cells = [tile_of(field, row, tile) for tile in range(level.tiles)]
    along = [tile_of(level.fy, row, tile) * (lane_above(cells, tile) - cells[tile]) for tile in range(level.tiles)]
    out = []
    for tile in range(level.tiles):
        here = cells[tile]
        deep = tile_of(level.fz, row, tile) * (depth_above(here) - here)
        value = tile_of(level.source, row, tile) - level.scale * tile_of(level.binding, row, tile) * here
        value = value + tile_of(level.fx, row, tile) * (tile_of(field, row + 1, tile) - here)
        value = value - tile_of(level.fx, row - 1, tile) * (here - tile_of(field, row - 1, tile))
        value = value + (along[tile] - lane_below(along, tile)) + (deep - depth_below(deep))
        out.append(value)
    return out


def relax(level, field, first, last, store, unrolled):
    def one(row):
        rest = residual(level, field, row)
        for tile in range(level.tiles):
            store(row, tile, tile_of(field, row, tile) + tile_of(level.weight, row, tile) * rest[tile])

    for_rows(first, last, one, unrolled)


def exact_dot(value, selector):
    high = value.astype(jnp.bfloat16)
    left = value - high.astype(F32)
    middle = left.astype(jnp.bfloat16)
    low = (left - middle.astype(F32)).astype(jnp.bfloat16)
    total = jnp.dot(low, selector, preferred_element_type=F32) + jnp.dot(middle, selector, preferred_element_type=F32)
    return total + jnp.dot(high, selector, preferred_element_type=F32)


def coarsen(tiles_in, coarse_tiles, select):
    out = []
    for tile in range(coarse_tiles):
        if 2 * tile + 1 < len(tiles_in):
            pair = jnp.concatenate([tiles_in[2 * tile], tiles_in[2 * tile + 1]], axis=1)
            out.append(exact_dot(pair, select[0]))
        else:
            out.append(exact_dot(tiles_in[2 * tile], select[1]))
    return out


def kernel(right_ref, conduct_ref, binding_ref, out_ref, *scratch):
    levels_refs, (staged, packed_fields, packed_source, local_sem, coarse_send, coarse_recv) = scratch[:-6], scratch[-6:]
    span_at, width_at = lax.axis_index("span"), lax.axis_index("width")
    plane, across = span_at // 4, lax.rem(span_at, 4)
    d0, sb0, db1, s1, db2, s2, db3, s3, db5, s5 = levels_refs[:10]
    rest = list(levels_refs[10:])

    def take():
        return rest.pop(0)

    base = (8 * span_at - 2, 4 * span_at - 2, 2 * span_at - 2, 4 * plane - 4, 2 * plane - 2, plane - 4)
    d4, b4, s4 = take(), take(), take()
    own = [
        (d0, sb0.at[1], sb0.at[0]),
        (db1.at[0], db1.at[1], s1),
        (db2.at[0], db2.at[1], s2),
        (db3.at[0], db3.at[1], s3),
        (d4, b4, s4),
        (db5.at[0], db5.at[1], s5),
    ]
    levels = [Level(i, own[i] + tuple(take() for _ in range(6)), base[i], width_at) for i in range(6)]
    sums = take()
    lifts = take()
    iterates = [take() for _ in range(6)]

    def device(across_span, across_width=0):
        return (lax.rem(span_at + (across_span + SPAN), SPAN), lax.rem(width_at + (across_width + WIDTH), WIDTH))

    ring = [(dz, dx) for dz in (0, 1, -1) for dx in range(4) if (dz, dx) != (0, 0)]

    def ring_device(dz, dx):
        to = lax.rem(across + dx, 4)
        return (lax.rem(4 * plane + (4 * dz + SPAN) + to, SPAN), width_at)

    around = [(1, 0), (-1, 0), (0, 1), (0, -1), (1, 1), (1, -1), (-1, 1), (-1, -1)]
    far = [(dz, 0) for dz in (2, -2, 3, -3, 4, -4)]

    barrier = pltpu.get_barrier_semaphore()
    partners = [ring_device(dz, dx) for dz, dx in ring] + [device(4 * dz) for dz, _ in far]
    partners += [device(a, b) for a, b in around if b != 0]
    for partner in partners:
        pl.semaphore_signal(barrier, inc=1, device_id=partner, device_id_type=MESH)

    inner = pl.ds(LANES, 4 * LANES)
    loads = []
    for i, (ref, target) in enumerate(((conduct_ref, d0), (right_ref, sb0.at[0]), (binding_ref, sb0.at[1]))):
        for row in range(8):
            loads.append(pltpu.make_async_copy(ref.at[:, row, :], target.at[2 + row, :, inner], local_sem.at[8 * i + row]))
            loads[-1].start()

    lane = lax.broadcasted_iota(jnp.int32, (2 * LANES, LANES), 0) // 2
    column = lax.broadcasted_iota(jnp.int32, (2 * LANES, LANES), 1)
    pair_select = jnp.where(lane == column, 0.25, 0.0).astype(jnp.bfloat16)
    lane = lax.broadcasted_iota(jnp.int32, (LANES, LANES), 0) // 2
    column = lax.broadcasted_iota(jnp.int32, (LANES, LANES), 1)
    twice_select = jnp.where(lane == lax.rem(column, LANES // 2), 0.25, 0.0).astype(jnp.bfloat16)
    select = (pair_select, twice_select)
    lane = lax.broadcasted_iota(jnp.int32, (LANES, LANES), 0)
    column = lax.broadcasted_iota(jnp.int32, (LANES, LANES), 1) // 2
    spread = tuple(jnp.where(lane == column + half * (LANES // 2), 1.0, 0.0).astype(jnp.bfloat16) for half in (0, 1))

    pl.semaphore_wait(barrier, len(partners))

    copies = []

    def send(source, target, to):
        at = len(copies)
        copy = pltpu.make_async_remote_copy(
            src_ref=source, dst_ref=target, send_sem=coarse_send.at[at], recv_sem=coarse_recv.at[at], device_id=to, device_id_type=MESH
        )
        copy.start()
        copies.append(copy)
        return copy

    def arrive(group):
        for copy in group:
            copy.wait_recv()

    first = []
    for to, near, second in ((1, 7, 6), (-1, 0, 1)):
        halo = 1 if to == 1 else 10
        first.append(send(conduct_ref.at[:, near, :], d0.at[halo, :, inner], device(to)))
        first.append(send(conduct_ref.at[:, second, :], d0.at[halo - to, :, inner], device(to)))
        first.append(send(right_ref.at[:, near, :], sb0.at[0, halo, :, inner], device(to)))
        first.append(send(binding_ref.at[:, near, :], sb0.at[1, halo, :, inner], device(to)))
    for load in loads[:8]:
        load.wait()

    def sideways(source, spans):
        for b in (1, -1):
            lanes_from, lanes_to = (pl.ds(4 * LANES, LANES), pl.ds(0, LANES)) if b == 1 else (pl.ds(LANES, LANES), pl.ds(5 * LANES, LANES))
            for a, rows_from, rows_to in spans:
                first.append(send(source.at[..., rows_from, :, lanes_from], source.at[..., rows_to, :, lanes_to], device(a, b)))

    sideways(d0, ((0, pl.ds(2, 8), pl.ds(2, 8)), (1, pl.ds(8, 2), pl.ds(0, 2)), (-1, pl.ds(2, 2), pl.ds(10, 2))))
    for load in loads[8:]:
        load.wait()
    for field in (sb0.at[0], sb0.at[1]):
        sideways(field, ((0, pl.ds(2, 8), pl.ds(2, 8)), (1, pl.ds(9, 1), pl.ds(1, 1)), (-1, pl.ds(2, 1), pl.ds(10, 1))))

    l0, l1, l2, l3, l4, l5 = levels
    factors_0, deep_0 = l0.y_factors(), l0.z_factor()

    def inside(row):
        face_x(l0, row, range(1, 5))
        face_y(l0, row, range(1, 4), factors_0)
        face_z(l0, row, range(1, 5), deep_0)

        @pl.when(row > 2)
        def _():
            weigh(l0, row, (2, 3))

    for_rows(2, 9, inside, False)
    face_y(l0, 9, range(1, 4), factors_0)
    face_z(l0, 9, range(1, 5), deep_0)
    arrive(first)

    def coarse_fields(fine, coarse, n_rows, fine_row, coarse_row, fill_rows=None):
        for pick_fine, pick_coarse in ((fine.conduct, coarse.conduct), (fine.binding, coarse.binding)):
            tiles = [
                jnp.concatenate([tile_of(pick_fine, fine_row + 2 * i, t) + tile_of(pick_fine, fine_row + 2 * i + 1, t) for i in range(n_rows)], axis=0)
                for t in range(fine.tiles)
            ]
            for t, value in enumerate(coarsen(tiles, coarse.tiles, select)):
                for i in range(n_rows):
                    put(pick_coarse, coarse_row + i, t, value[i * NZ : (i + 1) * NZ])

    def coarse_source(fine, coarse, n_rows, fine_row, coarse_row, unrolled):
        def one(i):
            low = residual(fine, fine.smooth, fine_row + 2 * i)
            high = residual(fine, fine.smooth, fine_row + 2 * i + 1)
            for t in range(fine.tiles):
                put(sums, i, t, low[t] + high[t])

        for_rows(0, n_rows, one, unrolled)
        tiles = [jnp.concatenate([tile_of(sums, i, t) for i in range(n_rows)], axis=0) for t in range(fine.tiles)]
        for t, value in enumerate(coarsen(tiles, coarse.tiles, select)):
            for i in range(n_rows):
                put(coarse.source, coarse_row + i, t, value[i * NZ : (i + 1) * NZ])

    def pack(value):
        lane = lax.broadcasted_iota(jnp.int32, (8, LANES), 1) // 32
        out = value[0:8]
        for group in range(1, 4):
            out = jnp.where(lane == group, pltpu.roll(value[8 * group : 8 * group + 8], 32 * group, 1), out)
        return out

    def unpack(value):
        return jnp.concatenate([value] + [pltpu.roll(value, LANES - 32 * group, 1) for group in range(1, 4)], axis=0)

    coarse_fields(l0, l1, 4, 2, 2)
    fields_1 = []
    for to, d_from, d_to, b_from, b_to in ((1, 4, 0, 5, 1), (-1, 2, 6, 2, 6)):
        fields_1.append(send(db1.at[0, pl.ds(d_from, 2)], db1.at[0, pl.ds(d_to, 2)], device(to)))
        fields_1.append(send(db1.at[1, pl.ds(b_from, 1)], db1.at[1, pl.ds(b_to, 1)], device(to)))

    def outside(row):
        face_x(l0, row, (0, 5))
        face_y(l0, row, (0, 4, 5), factors_0)
        face_z(l0, row, (0, 5), deep_0)

    for row in (0, 1, 9, 10):
        face_x(l0, row, range(6))
    for row in (1, 10):
        face_y(l0, row, range(6), factors_0)
        face_z(l0, row, range(6), deep_0)

    def weigh_rim(row):
        outside(row)
        weigh(l0, row, (0, 1, 4, 5))

    outside(2)
    for_rows(3, 9, weigh_rim, False)
    outside(9)
    for row in (1, 2, 9, 10):
        weigh(l0, row, range(6))
    smooth(l0, 1, 11, False)
    coarse_source(l0, l1, 4, 2, 2, False)

    sources_1 = [send(s1.at[pl.ds(5, 1)], s1.at[pl.ds(1, 1)], device(1)), send(s1.at[pl.ds(2, 1)], s1.at[pl.ds(6, 1)], device(-1))]

    coarse_fields(l1, l2, 2, 2, 2)
    fields_2 = []
    for to, d_from, d_to, b_from, b_to in ((1, 2, 0, 3, 1), (-1, 2, 4, 2, 4)):
        fields_2.append(send(db2.at[0, pl.ds(d_from, 2)], db2.at[0, pl.ds(d_to, 2)], device(to)))
        fields_2.append(send(db2.at[1, pl.ds(b_from, 1)], db2.at[1, pl.ds(b_to, 1)], device(to)))
    mine = 4 + across
    coarse_fields(l2, l3, 1, 2, mine)
    fields_3 = [
        send(db3.at[:, pl.ds(mine, 1)], db3.at[:, pl.ds(4 * (1 - dz) + across, 1)], ring_device(dz, dx)) for dz, dx in ring
    ]
    arrive(fields_1)
    faces(l1, 1, 7, False)
    arrive(sources_1)
    smooth(l1, 1, 7, False)
    coarse_source(l1, l2, 2, 2, 2, False)

    sources_2 = [send(s2.at[pl.ds(3, 1)], s2.at[pl.ds(1, 1)], device(1)), send(s2.at[pl.ds(2, 1)], s2.at[pl.ds(4, 1)], device(-1))]
    smooths_1 = [send(l1.smooth.at[pl.ds(4, 1)], l1.smooth.at[pl.ds(0, 1)], device(1)), send(l1.smooth.at[pl.ds(3, 1)], l1.smooth.at[pl.ds(7, 1)], device(-1))]
    arrive(fields_2)
    faces(l2, 1, 5, True)
    arrive(sources_2)
    smooth(l2, 1, 5, True)
    coarse_source(l2, l3, 1, 2, mine, True)

    sources_3 = [
        send(s3.at[pl.ds(mine, 1)], s3.at[pl.ds(4 * (1 - dz) + across, 1)], ring_device(dz, dx)) for dz, dx in ring
    ]
    smooths_2 = [send(l2.smooth.at[pl.ds(2, 1)], l2.smooth.at[pl.ds(0, 1)], device(1)), send(l2.smooth.at[pl.ds(3, 1)], l2.smooth.at[pl.ds(5, 1)], device(-1))]
    arrive(fields_3)
    coarse_fields(l3, l4, 6, 0, 0)
    coarse_fields(l4, l5, 1, 2, 4)
    for i in range(2):
        packed_fields[i, 4] = pack(db5[i, 4])
    fields_5 = [
        send(packed_fields.at[:, pl.ds(4, 1)], packed_fields.at[:, pl.ds(4 - dz, 1)], device(4 * dz)) for dz in (1, -1, 2, -2, 3, -3, 4, -4)
    ]
    faces(l3, 1, 11, False)
    faces(l4, 1, 5, True)
    arrive(sources_3)
    smooth(l3, 1, 11, True)
    coarse_source(l3, l4, 4, 2, 1, False)
    smooth(l4, 1, 5, True)
    coarse_source(l4, l5, 1, 2, 4, True)

    packed_source[4] = pack(s5[4])
    sources_5 = [send(packed_source.at[pl.ds(4, 1)], packed_source.at[pl.ds(4 - dz, 1)], device(4 * dz)) for dz in (1, -1, 2, -2, 3, -3)]
    smooths_4 = [send(l4.smooth.at[pl.ds(2, 1)], l4.smooth.at[pl.ds(0, 1)], device(4)), send(l4.smooth.at[pl.ds(3, 1)], l4.smooth.at[pl.ds(5, 1)], device(-4))]
    arrive(fields_5)
    for row in (0, 1, 2, 3, 5, 6, 7, 8):
        for i in range(2):
            db5[i, row] = unpack(packed_fields[i, row])
    faces(l5, 1, 8, True)
    arrive(sources_5)
    for row in (1, 2, 3, 5, 6, 7):
        s5[row] = unpack(packed_source[row])

    smooth(l5, 1, 8, True)

    def into(ref):
        return lambda row, tile, value: put(ref, row, tile, value)

    relax(l5, l5.smooth, 2, 7, into(l5.work), True)
    relax(l5, l5.work, 3, 6, into(iterates[5]), True)

    def lift(fine, coarse_ref, coarse_rows, coarse_tiles, first_row, last_row, coarse_of):
        values = [jnp.concatenate([tile_of(coarse_ref, c, t) for c in coarse_rows], axis=0) for t in range(coarse_tiles)]
        for t in range(fine.tiles):
            spread_out = exact_dot(values[t // 2], spread[t % 2])
            for row in range(first_row, last_row):
                at = coarse_of(row)
                put(lifts, row, t, tile_of(fine.smooth, row, t) + spread_out[at * NZ : (at + 1) * NZ])

    arrive(smooths_4)
    lift(l4, iterates[5], range(3, 6), 1, 0, 6, lambda row: row // 2)
    relax(l4, lifts, 1, 5, into(iterates[4]), True)
    lift(l3, iterates[4], range(1, 5), 1, 2, 10, lambda row: row // 2 - 1)
    relax(l3, lifts, 3, 9, into(iterates[3]), True)
    arrive(smooths_2)
    lift(l2, iterates[3], [across + 3 + i for i in range(3)], 1, 0, 6, lambda row: row // 2)
    relax(l2, lifts, 1, 5, into(iterates[2]), True)
    arrive(smooths_1)
    lift(l1, iterates[2], range(1, 5), 2, 0, 8, lambda row: row // 2)
    relax(l1, lifts, 1, 7, into(iterates[1]), False)
    lift(l0, iterates[1], range(1, 7), 3, 1, 11, lambda row: (row - 2) // 2 + 1)

    def finish(row, tile, value):
        if 1 <= tile <= 4:
            put(staged, row - 2, tile - 1, value)

    relax(l0, lifts, 2, 10, finish, False)
    stores = []
    for row in range(8):
        stores.append(pltpu.make_async_copy(staged.at[row], out_ref.at[:, row, :], local_sem.at[row]))
        stores[-1].start()
    for copy in stores:
        copy.wait()
    for copy in copies:
        copy.wait_send()


def shapes():
    def rows(level, *lead):
        return pltpu.VMEM((*lead, ROWS[level], NZ, TILES[level] * LANES), F32)

    first = [rows(0), rows(0, 2), rows(1, 2), rows(1), rows(2, 2), rows(2), rows(3, 2), rows(3), rows(5, 2), rows(5)]
    first += [rows(4), rows(4), rows(4)]
    for level in range(6):
        first += [rows(level) for _ in range(6)]
    first += [pltpu.VMEM((4, NZ, TILES[0] * LANES), F32), pltpu.VMEM((12, NZ, TILES[0] * LANES), F32)]
    first += [rows(level) for level in range(6)]
    first += [pltpu.VMEM((8, NZ, 512), F32), pltpu.VMEM((2, 9, 8, LANES), F32), pltpu.VMEM((9, 8, LANES), F32), pltpu.SemaphoreType.DMA((24,))]
    return first + [pltpu.SemaphoreType.DMA((N_SEMS,)), pltpu.SemaphoreType.DMA((N_SEMS,))]


def on_device(right_side, diffusivity, reaction):
    return pl.pallas_call(
        kernel,
        out_shape=jax.ShapeDtypeStruct((NZ, 8, 512), F32),
        in_specs=[pl.BlockSpec(memory_space=pl.ANY)] * 3,
        out_specs=pl.BlockSpec(memory_space=pl.ANY),
        scratch_shapes=shapes(),
        compiler_params=pltpu.CompilerParams(collective_id=0, has_side_effects=True, vmem_limit_bytes=VMEM_BYTES),
    )(right_side, diffusivity, reaction)


def solution(mesh):
    specs = P(None, "span", "width")
    return jax.shard_map(on_device, mesh=mesh, in_specs=(specs,) * 3, out_specs=specs, check_vma=False)
```

```python
import jax
import jax.numpy as jnp
from jax import lax
from jax.experimental import pallas as pl
from jax.experimental.pallas import tpu as pltpu
from jax.sharding import PartitionSpec as P


MESH = pl.DeviceIdType.MESH
F32 = jnp.float32
WEIGHT = 0.8
NZ = 32
LANES = 128
SPAN = 64
WIDTH = 8
ROWS = (12, 8, 6, 12, 6, 9)
TILES = (6, 3, 2, 1, 1, 1)
GRID_ROWS = (512, 256, 128, 64, 32, 16)
N_SEMS = 96
VMEM_BYTES = 62 << 20


class Level:
    def __init__(self, index, refs, base, width_at):
        self.index, self.base, self.width_at = index, base, width_at
        self.tiles = TILES[index]
        self.conduct, self.binding, self.source, self.smooth, self.fx, self.fy, self.fz, self.weight, self.work = refs
        self.scale = 0.25**index

    def cut(self, row):
        at = lax.rem(self.base + (row + 1 + GRID_ROWS[self.index]), GRID_ROWS[self.index])
        return jnp.where(at == 0, 0.0, 2.0 * self.scale).astype(F32)

    def y_factor(self, tile):
        halo, own = LANES >> self.index, 512 >> self.index
        low, high = halo - 1, halo + own - 1
        full = jnp.full((NZ, LANES), 2.0 * self.scale, F32)
        lane = lax.broadcasted_iota(jnp.int32, (NZ, LANES), 1)
        for place, edge in ((low, 0), (high, WIDTH - 1)):
            if place // LANES == tile:
                spot = jnp.where(self.width_at == edge, place % LANES, -1)
                full = jnp.where(lane == spot, 0.0, full)
        return full

    def y_factors(self):
        return [self.y_factor(tile) for tile in range(self.tiles)]

    def z_factor(self):
        depth = lax.broadcasted_iota(jnp.int32, (NZ, LANES), 0)
        return jnp.where(depth == NZ - 1, 0.0, 2.0 * self.scale)


def tile_of(ref, row, tile):
    return ref[row, :, pl.ds(tile * LANES, LANES)]


def put(ref, row, tile, value):
    ref[row, :, pl.ds(tile * LANES, LANES)] = value


def for_rows(first, last, body, unrolled):
    if unrolled:
        for row in range(first, last):
            body(row)
    else:
        lax.fori_loop(first, last, lambda row, carry: (body(row), carry)[1], 0, unroll=2 if (last - first) % 2 == 0 else 1)


def lane_above(tiles, tile):
    here = tiles[tile]
    after = tiles[min(tile + 1, len(tiles) - 1)]
    lane = lax.broadcasted_iota(jnp.int32, here.shape, 1)
    return pltpu.roll(jnp.where(lane == 0, after, here), LANES - 1, 1)


def lane_below(tiles, tile):
    here = tiles[tile]
    before = tiles[max(tile - 1, 0)]
    lane = lax.broadcasted_iota(jnp.int32, here.shape, 1)
    return pltpu.roll(jnp.where(lane == LANES - 1, before, here), 1, 1)


def depth_above(value):
    return pltpu.roll(value, NZ - 1, 0)


def depth_below(value):
    return pltpu.roll(value, 1, 0)


def mean_face(factor, first, second):
    return factor * (first * second) / (first + second)


def face_x(level, row, tiles):
    factor = level.cut(row)
    for tile in tiles:
        put(level.fx, row, tile, mean_face(factor, tile_of(level.conduct, row, tile), tile_of(level.conduct, row + 1, tile)))


def face_y(level, row, tiles, factors):
    for tile in tiles:
        near = {t: tile_of(level.conduct, row, t) for t in {tile, min(tile + 1, level.tiles - 1)}}
        after = near[min(tile + 1, level.tiles - 1)]
        put(level.fy, row, tile, mean_face(factors[tile], near[tile], lane_above((near[tile], after), 0)))


def face_z(level, row, tiles, factor):
    for tile in tiles:
        here = tile_of(level.conduct, row, tile)
        put(level.fz, row, tile, mean_face(factor, here, depth_above(here)))


def weigh(level, row, tiles):
    for tile in tiles:
        beside, deep = tile_of(level.fy, row, tile), tile_of(level.fz, row, tile)
        before = tile_of(level.fy, row, max(tile - 1, 0))
        diagonal = tile_of(level.fx, row - 1, tile) + tile_of(level.fx, row, tile)
        diagonal = diagonal + lane_below((before, beside), 1) + beside
        diagonal = diagonal + depth_below(deep) + deep + level.scale * tile_of(level.binding, row, tile)
        put(level.weight, row, tile, WEIGHT / diagonal)


def faces(level, first, last, unrolled):
    tiles = range(level.tiles)
    factors, deep_factor = level.y_factors(), level.z_factor()

    def one(row):
        face_x(level, row, tiles)
        face_y(level, row, tiles, factors)
        face_z(level, row, tiles, deep_factor)
        weigh(level, row, tiles)

    face_x(level, first - 1, tiles)
    for_rows(first, last, one, unrolled)


def smooth(level, first, last, unrolled):
    def one(row):
        for tile in range(level.tiles):
            put(level.smooth, row, tile, tile_of(level.weight, row, tile) * tile_of(level.source, row, tile))

    for_rows(first, last, one, unrolled)


def residual(level, field, row, wanted=None):
    wanted = wanted or range(level.tiles)
    cells = [tile_of(field, row, tile) for tile in range(level.tiles)]
    along = {
        tile: tile_of(level.fy, row, tile) * (lane_above(cells, tile) - cells[tile])
        for tile in range(max(wanted[0] - 1, 0), wanted[-1] + 1)
    }
    out = []
    for tile in wanted:
        here = cells[tile]
        deep = tile_of(level.fz, row, tile) * (depth_above(here) - here)
        value = tile_of(level.source, row, tile) - level.scale * tile_of(level.binding, row, tile) * here
        value = value + tile_of(level.fx, row, tile) * (tile_of(field, row + 1, tile) - here)
        value = value - tile_of(level.fx, row - 1, tile) * (here - tile_of(field, row - 1, tile))
        value = value + (along[tile] - lane_below(along, tile)) + (deep - depth_below(deep))
        out.append(value)
    return out


def relax(level, field, first, last, store, unrolled, wanted=None):
    def one(row):
        wanted_tiles = wanted or range(level.tiles)
        for tile, rest in zip(wanted_tiles, residual(level, field, row, wanted)):
            store(row, tile, tile_of(field, row, tile) + tile_of(level.weight, row, tile) * rest)

    for_rows(first, last, one, unrolled)


def exact_dot(value, selector):
    high = value.astype(jnp.bfloat16)
    left = value - high.astype(F32)
    middle = left.astype(jnp.bfloat16)
    low = (left - middle.astype(F32)).astype(jnp.bfloat16)
    total = jnp.dot(low, selector, preferred_element_type=F32) + jnp.dot(middle, selector, preferred_element_type=F32)
    return total + jnp.dot(high, selector, preferred_element_type=F32)


def coarsen(tiles_in, coarse_tiles, select):
    out = []
    for tile in range(coarse_tiles):
        if 2 * tile + 1 < len(tiles_in):
            pair = jnp.concatenate([tiles_in[2 * tile], tiles_in[2 * tile + 1]], axis=1)
            out.append(exact_dot(pair, select[0]))
        else:
            out.append(exact_dot(tiles_in[2 * tile], select[1]))
    return out


def kernel(right_ref, conduct_ref, binding_ref, out_ref, *scratch):
    levels_refs, (staged, packed_fields, packed_source, local_sem, coarse_send, coarse_recv) = scratch[:-6], scratch[-6:]
    span_at, width_at = lax.axis_index("span"), lax.axis_index("width")
    plane, across = span_at // 4, lax.rem(span_at, 4)
    d0, sb0, db1, s1, db2, s2, db3, s3, db5, s5 = levels_refs[:10]
    rest = list(levels_refs[10:])

    def take():
        return rest.pop(0)

    base = (8 * span_at - 2, 4 * span_at - 2, 2 * span_at - 2, 4 * plane - 4, 2 * plane - 2, plane - 4)
    d4, b4, s4 = take(), take(), take()
    own = [
        (d0, sb0.at[1], sb0.at[0]),
        (db1.at[0], db1.at[1], s1),
        (db2.at[0], db2.at[1], s2),
        (db3.at[0], db3.at[1], s3),
        (d4, b4, s4),
        (db5.at[0], db5.at[1], s5),
    ]
    levels = [Level(i, own[i] + tuple(take() for _ in range(6)), base[i], width_at) for i in range(6)]
    sums = take()
    lifts = take()
    iterates = [take() for _ in range(6)]

    def device(across_span, across_width=0):
        return (lax.rem(span_at + (across_span + SPAN), SPAN), lax.rem(width_at + (across_width + WIDTH), WIDTH))

    ring = [(dz, dx) for dz in (0, 1, -1) for dx in range(4) if (dz, dx) != (0, 0)]

    def ring_device(dz, dx):
        to = lax.rem(across + dx, 4)
        return (lax.rem(4 * plane + (4 * dz + SPAN) + to, SPAN), width_at)

    around = [(1, 0), (-1, 0), (0, 1), (0, -1), (1, 1), (1, -1), (-1, 1), (-1, -1)]
    far = [(dz, 0) for dz in (2, -2, 3, -3, 4, -4)]

    barrier = pltpu.get_barrier_semaphore()
    partners = [device(a, b) for a, b in around if b != 0]
    partners += [ring_device(dz, dx) for dz, dx in ring] + [device(4 * dz) for dz, _ in far]
    for partner in partners:
        pl.semaphore_signal(barrier, inc=1, device_id=partner, device_id_type=MESH)

    inner = pl.ds(LANES, 4 * LANES)
    loads = []
    for i, (ref, target) in enumerate(((conduct_ref, d0), (right_ref, sb0.at[0]), (binding_ref, sb0.at[1]))):
        for row in range(8):
            loads.append(pltpu.make_async_copy(ref.at[:, row, :], target.at[2 + row, :, inner], local_sem.at[8 * i + row]))
            loads[-1].start()

    lane = lax.broadcasted_iota(jnp.int32, (2 * LANES, LANES), 0) // 2
    column = lax.broadcasted_iota(jnp.int32, (2 * LANES, LANES), 1)
    pair_select = jnp.where(lane == column, 0.25, 0.0).astype(jnp.bfloat16)
    lane = lax.broadcasted_iota(jnp.int32, (LANES, LANES), 0) // 2
    column = lax.broadcasted_iota(jnp.int32, (LANES, LANES), 1)
    twice_select = jnp.where(lane == lax.rem(column, LANES // 2), 0.25, 0.0).astype(jnp.bfloat16)
    select = (pair_select, twice_select)
    lane = lax.broadcasted_iota(jnp.int32, (LANES, LANES), 0)
    column = lax.broadcasted_iota(jnp.int32, (LANES, LANES), 1) // 2
    spread = tuple(jnp.where(lane == column + half * (LANES // 2), 1.0, 0.0).astype(jnp.bfloat16) for half in (0, 1))

    pl.semaphore_wait(barrier, len(partners))

    copies = []

    def send(source, target, to):
        at = len(copies)
        copy = pltpu.make_async_remote_copy(
            src_ref=source, dst_ref=target, send_sem=coarse_send.at[at], recv_sem=coarse_recv.at[at], device_id=to, device_id_type=MESH
        )
        copy.start()
        copies.append(copy)
        return copy

    def arrive(group):
        for copy in group:
            copy.wait_recv()

    first = []
    for to, near, second in ((1, 7, 6), (-1, 0, 1)):
        halo = 1 if to == 1 else 10
        first.append(send(conduct_ref.at[:, near, :], d0.at[halo, :, inner], device(to)))
        first.append(send(conduct_ref.at[:, second, :], d0.at[halo - to, :, inner], device(to)))
        first.append(send(right_ref.at[:, near, :], sb0.at[0, halo, :, inner], device(to)))
        first.append(send(binding_ref.at[:, near, :], sb0.at[1, halo, :, inner], device(to)))
    for load in loads[:8]:
        load.wait()

    def sideways(source, spans):
        for b in (1, -1):
            lanes_from, lanes_to = (pl.ds(4 * LANES, LANES), pl.ds(0, LANES)) if b == 1 else (pl.ds(LANES, LANES), pl.ds(5 * LANES, LANES))
            for a, rows_from, rows_to in spans:
                first.append(send(source.at[..., rows_from, :, lanes_from], source.at[..., rows_to, :, lanes_to], device(a, b)))

    sideways(d0, ((0, pl.ds(2, 8), pl.ds(2, 8)), (1, pl.ds(8, 2), pl.ds(0, 2)), (-1, pl.ds(2, 2), pl.ds(10, 2))))
    for load in loads[8:]:
        load.wait()
    for field in (sb0.at[0], sb0.at[1]):
        sideways(field, ((0, pl.ds(2, 8), pl.ds(2, 8)), (1, pl.ds(9, 1), pl.ds(1, 1)), (-1, pl.ds(2, 1), pl.ds(10, 1))))

    l0, l1, l2, l3, l4, l5 = levels
    factors_0, deep_0 = l0.y_factors(), l0.z_factor()

    def inside(row):
        face_x(l0, row, range(1, 5))
        face_y(l0, row, range(1, 4), factors_0)
        face_z(l0, row, range(1, 5), deep_0)

        @pl.when(row > 2)
        def _():
            weigh(l0, row, (2, 3))

    for_rows(2, 9, inside, False)
    face_y(l0, 9, range(1, 4), factors_0)
    face_z(l0, 9, range(1, 5), deep_0)
    arrive(first)

    def coarse_field(fine, coarse, n_rows, fine_row, coarse_row):
        tiles = [
            jnp.concatenate([tile_of(fine[0], fine_row + 2 * i, t) + tile_of(fine[0], fine_row + 2 * i + 1, t) for i in range(n_rows)], axis=0)
            for t in range(fine[1])
        ]
        for t, value in enumerate(coarsen(tiles, coarse[1], select)):
            for i in range(n_rows):
                put(coarse[0], coarse_row + i, t, value[i * NZ : (i + 1) * NZ])

    def coarse_conduct(fine, coarse, n_rows, fine_row, coarse_row):
        coarse_field((fine.conduct, fine.tiles), (coarse.conduct, coarse.tiles), n_rows, fine_row, coarse_row)

    def coarse_binding(fine, coarse, n_rows, fine_row, coarse_row):
        coarse_field((fine.binding, fine.tiles), (coarse.binding, coarse.tiles), n_rows, fine_row, coarse_row)

    def coarse_fields(fine, coarse, n_rows, fine_row, coarse_row):
        coarse_conduct(fine, coarse, n_rows, fine_row, coarse_row)
        coarse_binding(fine, coarse, n_rows, fine_row, coarse_row)

    def coarse_source(fine, coarse, n_rows, fine_row, coarse_row, unrolled):
        def one(i):
            low = residual(fine, fine.smooth, fine_row + 2 * i)
            high = residual(fine, fine.smooth, fine_row + 2 * i + 1)
            for t in range(fine.tiles):
                put(sums, i, t, low[t] + high[t])

        for_rows(0, n_rows, one, unrolled)
        tiles = [jnp.concatenate([tile_of(sums, i, t) for i in range(n_rows)], axis=0) for t in range(fine.tiles)]
        for t, value in enumerate(coarsen(tiles, coarse.tiles, select)):
            for i in range(n_rows):
                put(coarse.source, coarse_row + i, t, value[i * NZ : (i + 1) * NZ])

    def pack(value):
        lane = lax.broadcasted_iota(jnp.int32, (8, LANES), 1) // 32
        out = value[0:8]
        for group in range(1, 4):
            out = jnp.where(lane == group, pltpu.roll(value[8 * group : 8 * group + 8], 32 * group, 1), out)
        return out

    def unpack(value):
        return jnp.concatenate([value] + [pltpu.roll(value, LANES - 32 * group, 1) for group in range(1, 4)], axis=0)

    coarse_conduct(l0, l1, 6, 0, 1)
    coarse_binding(l0, l1, 4, 2, 2)
    fields_1 = []
    for to, d_from, d_to, b_from, b_to in ((1, 4, 0, 5, 1), (-1, 3, 7, 2, 6)):
        fields_1.append(send(db1.at[0, pl.ds(d_from, 1)], db1.at[0, pl.ds(d_to, 1)], device(to)))
        fields_1.append(send(db1.at[1, pl.ds(b_from, 1)], db1.at[1, pl.ds(b_to, 1)], device(to)))

    def outside(row):
        face_x(l0, row, (0, 5))
        face_y(l0, row, (0, 4, 5), factors_0)
        face_z(l0, row, (0, 5), deep_0)

    for row in (0, 1, 9, 10):
        face_x(l0, row, range(6))
    for row in (1, 10):
        face_y(l0, row, range(6), factors_0)
        face_z(l0, row, range(6), deep_0)

    def weigh_rim(row):
        outside(row)
        weigh(l0, row, (0, 1, 4, 5))

    outside(2)
    for_rows(3, 9, weigh_rim, False)
    outside(9)
    for row in (1, 2, 9, 10):
        weigh(l0, row, range(6))
    smooth(l0, 1, 11, False)
    coarse_source(l0, l1, 4, 2, 2, False)

    sources_1 = [send(s1.at[pl.ds(5, 1)], s1.at[pl.ds(1, 1)], device(1)), send(s1.at[pl.ds(2, 1)], s1.at[pl.ds(6, 1)], device(-1))]

    coarse_fields(l1, l2, 2, 2, 2)
    fields_2 = []
    for to, d_from, d_to, b_from, b_to in ((1, 2, 0, 3, 1), (-1, 3, 5, 2, 4)):
        fields_2.append(send(db2.at[0, pl.ds(d_from, 1)], db2.at[0, pl.ds(d_to, 1)], device(to)))
        fields_2.append(send(db2.at[1, pl.ds(b_from, 1)], db2.at[1, pl.ds(b_to, 1)], device(to)))
    factors_1, deep_1 = l1.y_factors(), l1.z_factor()
    for row in (2, 3, 4, 5):
        face_y(l1, row, range(3), factors_1)
        face_z(l1, row, range(3), deep_1)
    for row in (1, 2, 3, 4, 5):
        face_x(l1, row, range(3))
    for row in (1, 6):
        face_y(l1, row, range(3), factors_1)
        face_z(l1, row, range(3), deep_1)
    for row in (3, 4):
        weigh(l1, row, range(3))
    mine = 4 + across
    coarse_fields(l2, l3, 1, 2, mine)
    arrive(fields_1)
    for row in (0, 6):
        face_x(l1, row, range(3))
    for row in (1, 2, 5, 6):
        weigh(l1, row, range(3))
    coarse_conduct(l1, l2, 1, 0, 1)
    coarse_conduct(l1, l2, 1, 6, 4)
    arrive(sources_1)
    smooth(l1, 1, 7, True)
    coarse_source(l1, l2, 2, 2, 2, True)

    sources_2 = [send(s2.at[pl.ds(3, 1)], s2.at[pl.ds(1, 1)], device(1)), send(s2.at[pl.ds(2, 1)], s2.at[pl.ds(4, 1)], device(-1))]
    smooths_1 = [send(l1.smooth.at[pl.ds(4, 1)], l1.smooth.at[pl.ds(0, 1)], device(1)), send(l1.smooth.at[pl.ds(3, 1)], l1.smooth.at[pl.ds(7, 1)], device(-1))]
    fields_3 = [
        send(db3.at[:, pl.ds(mine, 1)], db3.at[:, pl.ds(4 * (1 - dz) + across, 1)], ring_device(dz, dx)) for dz, dx in ring
    ]
    arrive(fields_2)
    faces(l2, 1, 5, True)
    arrive(sources_2)
    smooth(l2, 1, 5, True)
    coarse_source(l2, l3, 1, 2, mine, True)

    sources_3 = [
        send(s3.at[pl.ds(mine, 1)], s3.at[pl.ds(4 * (1 - dz) + across, 1)], ring_device(dz, dx)) for dz, dx in ring
    ]
    smooths_2 = [send(l2.smooth.at[pl.ds(2, 1)], l2.smooth.at[pl.ds(0, 1)], device(1)), send(l2.smooth.at[pl.ds(3, 1)], l2.smooth.at[pl.ds(5, 1)], device(-1))]
    arrive(fields_3)
    coarse_fields(l3, l4, 6, 0, 0)
    coarse_fields(l4, l5, 1, 2, 4)
    for i in range(2):
        packed_fields[i, 4] = pack(db5[i, 4])
    fields_5 = [
        send(packed_fields.at[:, pl.ds(4, 1)], packed_fields.at[:, pl.ds(4 - dz, 1)], device(4 * dz)) for dz in (1, -1, 2, -2, 3, -3, 4, -4)
    ]
    faces(l3, 1, 11, False)
    faces(l4, 1, 5, True)
    arrive(sources_3)
    smooth(l3, 1, 11, True)
    coarse_source(l3, l4, 4, 2, 1, True)
    smooth(l4, 1, 5, True)
    coarse_source(l4, l5, 1, 2, 4, True)

    packed_source[4] = pack(s5[4])
    sources_5 = [send(packed_source.at[pl.ds(4, 1)], packed_source.at[pl.ds(4 - dz, 1)], device(4 * dz)) for dz in (1, -1, 2, -2, 3, -3)]
    smooths_4 = [send(l4.smooth.at[pl.ds(2, 1)], l4.smooth.at[pl.ds(0, 1)], device(4)), send(l4.smooth.at[pl.ds(3, 1)], l4.smooth.at[pl.ds(5, 1)], device(-4))]
    arrive(fields_5)
    for row in (0, 1, 2, 3, 5, 6, 7, 8):
        for i in range(2):
            db5[i, row] = unpack(packed_fields[i, row])
    faces(l5, 1, 8, True)
    arrive(sources_5)
    for row in (1, 2, 3, 5, 6, 7):
        s5[row] = unpack(packed_source[row])

    smooth(l5, 1, 8, True)

    def into(ref):
        return lambda row, tile, value: put(ref, row, tile, value)

    relax(l5, l5.smooth, 2, 7, into(l5.work), True)
    relax(l5, l5.work, 3, 6, into(iterates[5]), True)

    def lift(fine, coarse_ref, coarse_rows, coarse_tiles, first_row, last_row, coarse_of):
        values = [jnp.concatenate([tile_of(coarse_ref, c, t) for c in coarse_rows], axis=0) for t in range(coarse_tiles)]
        for t in range(fine.tiles):
            spread_out = exact_dot(values[t // 2], spread[t % 2])
            for row in range(first_row, last_row):
                at = coarse_of(row)
                put(lifts, row, t, tile_of(fine.smooth, row, t) + spread_out[at * NZ : (at + 1) * NZ])

    arrive(smooths_4)
    lift(l4, iterates[5], range(3, 6), 1, 0, 6, lambda row: row // 2)
    relax(l4, lifts, 1, 5, into(iterates[4]), True)
    lift(l3, iterates[4], range(1, 5), 1, 2, 10, lambda row: row // 2 - 1)
    relax(l3, lifts, 3, 9, into(iterates[3]), True)
    arrive(smooths_2)
    lift(l2, iterates[3], [across + 3 + i for i in range(3)], 1, 0, 6, lambda row: row // 2)
    relax(l2, lifts, 1, 5, into(iterates[2]), True)
    arrive(smooths_1)
    lift(l1, iterates[2], range(1, 5), 2, 0, 8, lambda row: row // 2)
    relax(l1, lifts, 1, 7, into(iterates[1]), True)
    lift(l0, iterates[1], range(1, 7), 3, 1, 11, lambda row: (row - 2) // 2 + 1)

    def finish(row, tile, value):
        put(staged, row - 2, tile - 1, value)

    relax(l0, lifts, 2, 10, finish, False, range(1, 5))
    stores = []
    for row in range(8):
        stores.append(pltpu.make_async_copy(staged.at[row], out_ref.at[:, row, :], local_sem.at[row]))
        stores[-1].start()
    for copy in stores:
        copy.wait()
    for copy in copies:
        copy.wait_send()


def shapes():
    def rows(level, *lead):
        return pltpu.VMEM((*lead, ROWS[level], NZ, TILES[level] * LANES), F32)

    first = [rows(0), rows(0, 2), rows(1, 2), rows(1), rows(2, 2), rows(2), rows(3, 2), rows(3), rows(5, 2), rows(5)]
    first += [rows(4), rows(4), rows(4)]
    for level in range(6):
        first += [rows(level) for _ in range(6)]
    first += [pltpu.VMEM((4, NZ, TILES[0] * LANES), F32), pltpu.VMEM((12, NZ, TILES[0] * LANES), F32)]
    first += [rows(level) for level in range(6)]
    first += [pltpu.VMEM((8, NZ, 512), F32), pltpu.VMEM((2, 9, 8, LANES), F32), pltpu.VMEM((9, 8, LANES), F32), pltpu.SemaphoreType.DMA((24,))]
    return first + [pltpu.SemaphoreType.DMA((N_SEMS,)), pltpu.SemaphoreType.DMA((N_SEMS,))]


def on_device(right_side, diffusivity, reaction):
    return pl.pallas_call(
        kernel,
        out_shape=jax.ShapeDtypeStruct((NZ, 8, 512), F32),
        in_specs=[pl.BlockSpec(memory_space=pl.ANY)] * 3,
        out_specs=pl.BlockSpec(memory_space=pl.ANY),
        scratch_shapes=shapes(),
        compiler_params=pltpu.CompilerParams(collective_id=0, has_side_effects=True, vmem_limit_bytes=VMEM_BYTES),
    )(right_side, diffusivity, reaction)


def solution(mesh):
    specs = P(None, "span", "width")
    return jax.shard_map(on_device, mesh=mesh, in_specs=(specs,) * 3, out_specs=specs, check_vma=False)
```

```python
import jax
import jax.numpy as jnp
from jax import lax
from jax.experimental import pallas as pl
from jax.experimental.pallas import tpu as pltpu
from jax.sharding import PartitionSpec as P


MESH = pl.DeviceIdType.MESH
F32 = jnp.float32
WEIGHT = 0.8
NZ = 32
LANES = 128
SPAN = 64
WIDTH = 8
ROWS = (12, 8, 6, 12, 6, 9)
TILES = (6, 3, 2, 1, 1, 1)
GRID_ROWS = (512, 256, 128, 64, 32, 16)
N_SEMS = 96
VMEM_BYTES = 62 << 20


class Level:
    def __init__(self, index, refs, base, width_at):
        self.index, self.base, self.width_at = index, base, width_at
        self.tiles = TILES[index]
        self.conduct, self.binding, self.source, self.smooth, self.fx, self.fy, self.fz, self.weight, self.work = refs
        self.scale = 0.25**index

    def cut(self, row):
        at = lax.rem(self.base + (row + 1 + GRID_ROWS[self.index]), GRID_ROWS[self.index])
        return jnp.where(at == 0, 0.0, 2.0 * self.scale).astype(F32)

    def y_factor(self, tile):
        halo, own = LANES >> self.index, 512 >> self.index
        low, high = halo - 1, halo + own - 1
        full = jnp.full((NZ, LANES), 2.0 * self.scale, F32)
        lane = lax.broadcasted_iota(jnp.int32, (NZ, LANES), 1)
        for place, edge in ((low, 0), (high, WIDTH - 1)):
            if place // LANES == tile:
                spot = jnp.where(self.width_at == edge, place % LANES, -1)
                full = jnp.where(lane == spot, 0.0, full)
        return full

    def y_factors(self):
        return [self.y_factor(tile) for tile in range(self.tiles)]

    def z_factor(self):
        depth = lax.broadcasted_iota(jnp.int32, (NZ, LANES), 0)
        return jnp.where(depth == NZ - 1, 0.0, 2.0 * self.scale)


def tile_of(ref, row, tile):
    return ref[row, :, pl.ds(tile * LANES, LANES)]


def put(ref, row, tile, value):
    ref[row, :, pl.ds(tile * LANES, LANES)] = value


def for_rows(first, last, body, unrolled):
    if unrolled:
        for row in range(first, last):
            body(row)
    else:
        lax.fori_loop(first, last, lambda row, carry: (body(row), carry)[1], 0, unroll=2 if (last - first) % 2 == 0 else 1)


def lane_above(tiles, tile):
    here = tiles[tile]
    after = tiles[min(tile + 1, len(tiles) - 1)]
    lane = lax.broadcasted_iota(jnp.int32, here.shape, 1)
    return pltpu.roll(jnp.where(lane == 0, after, here), LANES - 1, 1)


def lane_below(tiles, tile):
    here = tiles[tile]
    before = tiles[max(tile - 1, 0)]
    lane = lax.broadcasted_iota(jnp.int32, here.shape, 1)
    return pltpu.roll(jnp.where(lane == LANES - 1, before, here), 1, 1)


def depth_above(value):
    return pltpu.roll(value, NZ - 1, 0)


def depth_below(value):
    return pltpu.roll(value, 1, 0)


def mean_face(factor, first, second):
    return factor * (first * second) / (first + second)


def face_x(level, row, tiles):
    factor = level.cut(row)
    for tile in tiles:
        put(level.fx, row, tile, mean_face(factor, tile_of(level.conduct, row, tile), tile_of(level.conduct, row + 1, tile)))


def face_y(level, row, tiles, factors):
    for tile in tiles:
        near = {t: tile_of(level.conduct, row, t) for t in {tile, min(tile + 1, level.tiles - 1)}}
        after = near[min(tile + 1, level.tiles - 1)]
        put(level.fy, row, tile, mean_face(factors[tile], near[tile], lane_above((near[tile], after), 0)))


def face_z(level, row, tiles, factor):
    for tile in tiles:
        here = tile_of(level.conduct, row, tile)
        put(level.fz, row, tile, mean_face(factor, here, depth_above(here)))


def weigh(level, row, tiles):
    for tile in tiles:
        beside, deep = tile_of(level.fy, row, tile), tile_of(level.fz, row, tile)
        before = tile_of(level.fy, row, max(tile - 1, 0))
        diagonal = tile_of(level.fx, row - 1, tile) + tile_of(level.fx, row, tile)
        diagonal = diagonal + lane_below((before, beside), 1) + beside
        diagonal = diagonal + depth_below(deep) + deep + level.scale * tile_of(level.binding, row, tile)
        put(level.weight, row, tile, WEIGHT / diagonal)


def faces(level, first, last, unrolled):
    tiles = range(level.tiles)
    factors, deep_factor = level.y_factors(), level.z_factor()

    def one(row):
        face_x(level, row, tiles)
        face_y(level, row, tiles, factors)
        face_z(level, row, tiles, deep_factor)
        weigh(level, row, tiles)

    face_x(level, first - 1, tiles)
    for_rows(first, last, one, unrolled)


def smooth(level, first, last, unrolled):
    def one(row):
        for tile in range(level.tiles):
            put(level.smooth, row, tile, tile_of(level.weight, row, tile) * tile_of(level.source, row, tile))

    for_rows(first, last, one, unrolled)


def residual(level, field, row, wanted=None):
    wanted = wanted or range(level.tiles)
    cells = [tile_of(field, row, tile) for tile in range(level.tiles)]
    along = {
        tile: tile_of(level.fy, row, tile) * (lane_above(cells, tile) - cells[tile])
        for tile in range(max(wanted[0] - 1, 0), wanted[-1] + 1)
    }
    out = []
    for tile in wanted:
        here = cells[tile]
        deep = tile_of(level.fz, row, tile) * (depth_above(here) - here)
        value = tile_of(level.source, row, tile) - level.scale * tile_of(level.binding, row, tile) * here
        value = value + tile_of(level.fx, row, tile) * (tile_of(field, row + 1, tile) - here)
        value = value - tile_of(level.fx, row - 1, tile) * (here - tile_of(field, row - 1, tile))
        value = value + (along[tile] - lane_below(along, tile)) + (deep - depth_below(deep))
        out.append(value)
    return out


def relax(level, field, first, last, store, unrolled, wanted=None):
    def one(row):
        wanted_tiles = wanted or range(level.tiles)
        for tile, rest in zip(wanted_tiles, residual(level, field, row, wanted)):
            store(row, tile, tile_of(field, row, tile) + tile_of(level.weight, row, tile) * rest)

    for_rows(first, last, one, unrolled)


def exact_dot(value, selector):
    high = value.astype(jnp.bfloat16)
    left = value - high.astype(F32)
    middle = left.astype(jnp.bfloat16)
    low = (left - middle.astype(F32)).astype(jnp.bfloat16)
    total = jnp.dot(low, selector, preferred_element_type=F32) + jnp.dot(middle, selector, preferred_element_type=F32)
    return total + jnp.dot(high, selector, preferred_element_type=F32)


def coarsen(tiles_in, coarse_tiles, select):
    out = []
    for tile in range(coarse_tiles):
        if 2 * tile + 1 < len(tiles_in):
            pair = jnp.concatenate([tiles_in[2 * tile], tiles_in[2 * tile + 1]], axis=1)
            out.append(exact_dot(pair, select[0]))
        else:
            out.append(exact_dot(tiles_in[2 * tile], select[1]))
    return out


def kernel(right_ref, conduct_ref, binding_ref, out_ref, *scratch):
    levels_refs, (staged, packed_fields, packed_source, local_sem, coarse_send, coarse_recv) = scratch[:-6], scratch[-6:]
    span_at, width_at = lax.axis_index("span"), lax.axis_index("width")
    plane, across = span_at // 4, lax.rem(span_at, 4)
    d0, sb0, db1, s1, db2, s2, db3, s3, db5, s5 = levels_refs[:10]
    rest = list(levels_refs[10:])

    def take():
        return rest.pop(0)

    base = (8 * span_at - 2, 4 * span_at - 2, 2 * span_at - 2, 4 * plane - 4, 2 * plane - 2, plane - 4)
    d4, b4, s4 = take(), take(), take()
    own = [
        (d0, sb0.at[1], sb0.at[0]),
        (db1.at[0], db1.at[1], s1),
        (db2.at[0], db2.at[1], s2),
        (db3.at[0], db3.at[1], s3),
        (d4, b4, s4),
        (db5.at[0], db5.at[1], s5),
    ]
    levels = [Level(i, own[i] + tuple(take() for _ in range(6)), base[i], width_at) for i in range(6)]
    sums = take()
    lifts = take()
    iterates = [take() for _ in range(6)]

    def device(across_span, across_width=0):
        return (lax.rem(span_at + (across_span + SPAN), SPAN), lax.rem(width_at + (across_width + WIDTH), WIDTH))

    ring = [(dz, dx) for dz in (0, 1, -1) for dx in range(4) if (dz, dx) != (0, 0)]

    def ring_device(dz, dx):
        to = lax.rem(across + dx, 4)
        return (lax.rem(4 * plane + (4 * dz + SPAN) + to, SPAN), width_at)

    around = [(1, 0), (-1, 0), (0, 1), (0, -1), (1, 1), (1, -1), (-1, 1), (-1, -1)]
    far = [(dz, 0) for dz in (2, -2, 3, -3, 4, -4)]

    barrier = pltpu.get_barrier_semaphore()
    partners = [device(a, b) for a, b in around if b != 0]
    partners += [ring_device(dz, dx) for dz, dx in ring] + [device(4 * dz) for dz, _ in far]
    for partner in partners:
        pl.semaphore_signal(barrier, inc=1, device_id=partner, device_id_type=MESH)

    inner = pl.ds(LANES, 4 * LANES)
    loads = []
    for i, (ref, target) in enumerate(((conduct_ref, d0), (binding_ref, sb0.at[1]), (right_ref, sb0.at[0]))):
        for row in range(8):
            loads.append(pltpu.make_async_copy(ref.at[:, row, :], target.at[2 + row, :, inner], local_sem.at[8 * i + row]))
            loads[-1].start()

    lane = lax.broadcasted_iota(jnp.int32, (2 * LANES, LANES), 0) // 2
    column = lax.broadcasted_iota(jnp.int32, (2 * LANES, LANES), 1)
    pair_select = jnp.where(lane == column, 0.25, 0.0).astype(jnp.bfloat16)
    lane = lax.broadcasted_iota(jnp.int32, (LANES, LANES), 0) // 2
    column = lax.broadcasted_iota(jnp.int32, (LANES, LANES), 1)
    twice_select = jnp.where(lane == lax.rem(column, LANES // 2), 0.25, 0.0).astype(jnp.bfloat16)
    select = (pair_select, twice_select)
    lane = lax.broadcasted_iota(jnp.int32, (LANES, LANES), 0)
    column = lax.broadcasted_iota(jnp.int32, (LANES, LANES), 1) // 2
    spread = tuple(jnp.where(lane == column + half * (LANES // 2), 1.0, 0.0).astype(jnp.bfloat16) for half in (0, 1))

    pl.semaphore_wait(barrier, len(partners))

    copies = []

    def send(source, target, to):
        at = len(copies)
        copy = pltpu.make_async_remote_copy(
            src_ref=source, dst_ref=target, send_sem=coarse_send.at[at], recv_sem=coarse_recv.at[at], device_id=to, device_id_type=MESH
        )
        copy.start()
        copies.append(copy)
        return copy

    def arrive(group):
        for copy in group:
            copy.wait_recv()

    for load in loads[:8]:
        load.wait()
    rows_d = [send(d0.at[pl.ds(8, 2), :, inner], d0.at[pl.ds(0, 2), :, inner], device(1)), send(d0.at[pl.ds(2, 2), :, inner], d0.at[pl.ds(10, 2), :, inner], device(-1))]
    def sideways(source, spans):
        sent = []
        for b in (1, -1):
            lanes_from, lanes_to = (pl.ds(4 * LANES, LANES), pl.ds(0, LANES)) if b == 1 else (pl.ds(LANES, LANES), pl.ds(5 * LANES, LANES))
            for a, rows_from, rows_to in spans:
                sent.append(send(source.at[rows_from, :, lanes_from], source.at[rows_to, :, lanes_to], device(a, b)))
        return sent

    beside = ((0, pl.ds(2, 8), pl.ds(2, 8)),)
    corner = ((1, pl.ds(9, 1), pl.ds(1, 1)), (-1, pl.ds(2, 1), pl.ds(10, 1)))
    lanes_d = sideways(d0, beside)
    corners_d = sideways(d0, ((1, pl.ds(8, 2), pl.ds(0, 2)), (-1, pl.ds(2, 2), pl.ds(10, 2))))
    for load in loads[8:16]:
        load.wait()
    rows_b = [send(sb0.at[1, pl.ds(9, 1), :, inner], sb0.at[1, pl.ds(1, 1), :, inner], device(1)), send(sb0.at[1, pl.ds(2, 1), :, inner], sb0.at[1, pl.ds(10, 1), :, inner], device(-1))]
    lanes_b = sideways(sb0.at[1], beside)
    corners_b = sideways(sb0.at[1], corner)
    for load in loads[16:]:
        load.wait()
    rows_s = [send(sb0.at[0, pl.ds(9, 1), :, inner], sb0.at[0, pl.ds(1, 1), :, inner], device(1)), send(sb0.at[0, pl.ds(2, 1), :, inner], sb0.at[0, pl.ds(10, 1), :, inner], device(-1))]
    lanes_s = sideways(sb0.at[0], beside)
    corners_s = sideways(sb0.at[0], corner)

    l0, l1, l2, l3, l4, l5 = levels
    factors_0, deep_0 = l0.y_factors(), l0.z_factor()

    def inside(row):
        face_x(l0, row, range(1, 5))
        face_y(l0, row, range(1, 4), factors_0)
        face_z(l0, row, range(1, 5), deep_0)

        @pl.when(row > 2)
        def _():
            weigh(l0, row, (2, 3))

    for_rows(2, 9, inside, False)
    face_y(l0, 9, range(1, 4), factors_0)
    face_z(l0, 9, range(1, 5), deep_0)

    arrive(rows_d)
    for row in (0, 1, 9, 10):
        face_x(l0, row, range(1, 5))
    for row in (1, 10):
        face_y(l0, row, range(1, 4), factors_0)
        face_z(l0, row, range(1, 5), deep_0)
    for row in (2, 9):
        weigh(l0, row, (2, 3))
    arrive(lanes_d)

    def outside(row):
        face_y(l0, row, (0, 4, 5), factors_0)
        face_z(l0, row, (0, 5), deep_0)

    def outside_x(row):
        outside(row)
        face_x(l0, row, (0, 5))

    for_rows(3, 9, outside_x, False)
    outside_x(2)
    outside(9)
    arrive(lanes_b)
    for_rows(3, 9, lambda row: weigh(l0, row, (0, 1, 4, 5)), False)
    for row in (2, 9):
        weigh(l0, row, (1, 4))
    arrive(rows_b)
    for row in (1, 10):
        weigh(l0, row, (2, 3))
    arrive(corners_d)
    for row in (0, 1, 9, 10):
        face_x(l0, row, (0, 5))
    for row in (1, 10):
        face_y(l0, row, (0, 4, 5), factors_0)
        face_z(l0, row, (0, 5), deep_0)
    arrive(corners_b)
    for row in (2, 9):
        weigh(l0, row, (0, 5))
    for row in (1, 10):
        weigh(l0, row, (0, 1, 4, 5))

    def coarse_field(fine, coarse, n_rows, fine_row, coarse_row):
        tiles = [
            jnp.concatenate([tile_of(fine[0], fine_row + 2 * i, t) + tile_of(fine[0], fine_row + 2 * i + 1, t) for i in range(n_rows)], axis=0)
            for t in range(fine[1])
        ]
        for t, value in enumerate(coarsen(tiles, coarse[1], select)):
            for i in range(n_rows):
                put(coarse[0], coarse_row + i, t, value[i * NZ : (i + 1) * NZ])

    def coarse_conduct(fine, coarse, n_rows, fine_row, coarse_row):
        coarse_field((fine.conduct, fine.tiles), (coarse.conduct, coarse.tiles), n_rows, fine_row, coarse_row)

    def coarse_binding(fine, coarse, n_rows, fine_row, coarse_row):
        coarse_field((fine.binding, fine.tiles), (coarse.binding, coarse.tiles), n_rows, fine_row, coarse_row)

    def coarse_fields(fine, coarse, n_rows, fine_row, coarse_row):
        coarse_conduct(fine, coarse, n_rows, fine_row, coarse_row)
        coarse_binding(fine, coarse, n_rows, fine_row, coarse_row)

    def coarse_source(fine, coarse, n_rows, fine_row, coarse_row, unrolled):
        def one(i):
            low = residual(fine, fine.smooth, fine_row + 2 * i)
            high = residual(fine, fine.smooth, fine_row + 2 * i + 1)
            for t in range(fine.tiles):
                put(sums, i, t, low[t] + high[t])

        for_rows(0, n_rows, one, unrolled)
        tiles = [jnp.concatenate([tile_of(sums, i, t) for i in range(n_rows)], axis=0) for t in range(fine.tiles)]
        for t, value in enumerate(coarsen(tiles, coarse.tiles, select)):
            for i in range(n_rows):
                put(coarse.source, coarse_row + i, t, value[i * NZ : (i + 1) * NZ])

    def pack(value):
        lane = lax.broadcasted_iota(jnp.int32, (8, LANES), 1) // 32
        out = value[0:8]
        for group in range(1, 4):
            out = jnp.where(lane == group, pltpu.roll(value[8 * group : 8 * group + 8], 32 * group, 1), out)
        return out

    def unpack(value):
        return jnp.concatenate([value] + [pltpu.roll(value, LANES - 32 * group, 1) for group in range(1, 4)], axis=0)

    coarse_conduct(l0, l1, 6, 0, 1)
    coarse_binding(l0, l1, 4, 2, 2)
    fields_1 = []
    for to, d_from, d_to, b_from, b_to in ((1, 4, 0, 5, 1), (-1, 3, 7, 2, 6)):
        fields_1.append(send(db1.at[0, pl.ds(d_from, 1)], db1.at[0, pl.ds(d_to, 1)], device(to)))
        fields_1.append(send(db1.at[1, pl.ds(b_from, 1)], db1.at[1, pl.ds(b_to, 1)], device(to)))

    arrive(rows_s + lanes_s + corners_s)
    smooth(l0, 1, 11, False)
    coarse_source(l0, l1, 4, 2, 2, False)

    sources_1 = [send(s1.at[pl.ds(5, 1)], s1.at[pl.ds(1, 1)], device(1)), send(s1.at[pl.ds(2, 1)], s1.at[pl.ds(6, 1)], device(-1))]

    coarse_fields(l1, l2, 2, 2, 2)
    fields_2 = []
    for to, d_from, d_to, b_from, b_to in ((1, 2, 0, 3, 1), (-1, 3, 5, 2, 4)):
        fields_2.append(send(db2.at[0, pl.ds(d_from, 1)], db2.at[0, pl.ds(d_to, 1)], device(to)))
        fields_2.append(send(db2.at[1, pl.ds(b_from, 1)], db2.at[1, pl.ds(b_to, 1)], device(to)))
    factors_1, deep_1 = l1.y_factors(), l1.z_factor()
    for row in (2, 3, 4, 5):
        face_y(l1, row, range(3), factors_1)
        face_z(l1, row, range(3), deep_1)
    for row in (1, 2, 3, 4, 5):
        face_x(l1, row, range(3))
    for row in (1, 6):
        face_y(l1, row, range(3), factors_1)
        face_z(l1, row, range(3), deep_1)
    for row in (3, 4):
        weigh(l1, row, range(3))
    mine = 4 + across
    coarse_fields(l2, l3, 1, 2, mine)
    arrive(fields_1)
    for row in (0, 6):
        face_x(l1, row, range(3))
    for row in (1, 2, 5, 6):
        weigh(l1, row, range(3))
    coarse_conduct(l1, l2, 1, 0, 1)
    coarse_conduct(l1, l2, 1, 6, 4)
    arrive(sources_1)
    smooth(l1, 1, 7, True)
    coarse_source(l1, l2, 2, 2, 2, True)

    sources_2 = [send(s2.at[pl.ds(3, 1)], s2.at[pl.ds(1, 1)], device(1)), send(s2.at[pl.ds(2, 1)], s2.at[pl.ds(4, 1)], device(-1))]
    smooths_1 = [send(l1.smooth.at[pl.ds(4, 1)], l1.smooth.at[pl.ds(0, 1)], device(1)), send(l1.smooth.at[pl.ds(3, 1)], l1.smooth.at[pl.ds(7, 1)], device(-1))]
    fields_3 = [
        send(db3.at[:, pl.ds(mine, 1)], db3.at[:, pl.ds(4 * (1 - dz) + across, 1)], ring_device(dz, dx)) for dz, dx in ring
    ]
    arrive(fields_2)
    faces(l2, 1, 5, True)
    arrive(sources_2)
    smooth(l2, 1, 5, True)
    coarse_source(l2, l3, 1, 2, mine, True)

    sources_3 = [
        send(s3.at[pl.ds(mine, 1)], s3.at[pl.ds(4 * (1 - dz) + across, 1)], ring_device(dz, dx)) for dz, dx in ring
    ]
    smooths_2 = [send(l2.smooth.at[pl.ds(2, 1)], l2.smooth.at[pl.ds(0, 1)], device(1)), send(l2.smooth.at[pl.ds(3, 1)], l2.smooth.at[pl.ds(5, 1)], device(-1))]
    arrive(fields_3)
    coarse_fields(l3, l4, 6, 0, 0)
    coarse_fields(l4, l5, 1, 2, 4)
    for i in range(2):
        packed_fields[i, 4] = pack(db5[i, 4])
    fields_5 = [
        send(packed_fields.at[:, pl.ds(4, 1)], packed_fields.at[:, pl.ds(4 - dz, 1)], device(4 * dz)) for dz in (1, -1, 2, -2, 3, -3, 4, -4)
    ]
    faces(l3, 1, 11, False)
    faces(l4, 1, 5, True)
    arrive(sources_3)
    smooth(l3, 1, 11, True)
    coarse_source(l3, l4, 4, 2, 1, True)
    smooth(l4, 1, 5, True)
    coarse_source(l4, l5, 1, 2, 4, True)

    packed_source[4] = pack(s5[4])
    sources_5 = [send(packed_source.at[pl.ds(4, 1)], packed_source.at[pl.ds(4 - dz, 1)], device(4 * dz)) for dz in (1, -1, 2, -2, 3, -3)]
    smooths_4 = [send(l4.smooth.at[pl.ds(2, 1)], l4.smooth.at[pl.ds(0, 1)], device(4)), send(l4.smooth.at[pl.ds(3, 1)], l4.smooth.at[pl.ds(5, 1)], device(-4))]
    arrive(fields_5)
    for row in (0, 1, 2, 3, 5, 6, 7, 8):
        for i in range(2):
            db5[i, row] = unpack(packed_fields[i, row])
    faces(l5, 1, 8, True)
    arrive(sources_5)
    for row in (1, 2, 3, 5, 6, 7):
        s5[row] = unpack(packed_source[row])

    smooth(l5, 1, 8, True)

    def into(ref):
        return lambda row, tile, value: put(ref, row, tile, value)

    relax(l5, l5.smooth, 2, 7, into(l5.work), True)
    relax(l5, l5.work, 3, 6, into(iterates[5]), True)

    def lift(fine, coarse_ref, coarse_rows, coarse_tiles, first_row, last_row, coarse_of):
        values = [jnp.concatenate([tile_of(coarse_ref, c, t) for c in coarse_rows], axis=0) for t in range(coarse_tiles)]
        for t in range(fine.tiles):
            spread_out = exact_dot(values[t // 2], spread[t % 2])
            for row in range(first_row, last_row):
                at = coarse_of(row)
                put(lifts, row, t, tile_of(fine.smooth, row, t) + spread_out[at * NZ : (at + 1) * NZ])

    arrive(smooths_4)
    lift(l4, iterates[5], range(3, 6), 1, 0, 6, lambda row: row // 2)
    relax(l4, lifts, 1, 5, into(iterates[4]), True)
    lift(l3, iterates[4], range(1, 5), 1, 2, 10, lambda row: row // 2 - 1)
    relax(l3, lifts, 3, 9, into(iterates[3]), True)
    arrive(smooths_2)
    lift(l2, iterates[3], [across + 3 + i for i in range(3)], 1, 0, 6, lambda row: row // 2)
    relax(l2, lifts, 1, 5, into(iterates[2]), True)
    arrive(smooths_1)
    lift(l1, iterates[2], range(1, 5), 2, 0, 8, lambda row: row // 2)
    relax(l1, lifts, 1, 7, into(iterates[1]), True)
    lift(l0, iterates[1], range(1, 7), 3, 1, 11, lambda row: (row - 2) // 2 + 1)

    stores = []

    def finish(row, tile, value):
        put(staged, row - 2, tile - 1, value)
        if tile == 4:
            stores.append(pltpu.make_async_copy(staged.at[row - 2], out_ref.at[:, row - 2, :], local_sem.at[row - 2]))
            stores[-1].start()

    relax(l0, lifts, 2, 10, finish, True, range(1, 5))
    for copy in stores:
        copy.wait()
    for copy in copies:
        copy.wait_send()


def shapes():
    def rows(level, *lead):
        return pltpu.VMEM((*lead, ROWS[level], NZ, TILES[level] * LANES), F32)

    first = [rows(0), rows(0, 2), rows(1, 2), rows(1), rows(2, 2), rows(2), rows(3, 2), rows(3), rows(5, 2), rows(5)]
    first += [rows(4), rows(4), rows(4)]
    for level in range(6):
        first += [rows(level) for _ in range(6)]
    first += [pltpu.VMEM((4, NZ, TILES[0] * LANES), F32), pltpu.VMEM((12, NZ, TILES[0] * LANES), F32)]
    first += [rows(level) for level in range(6)]
    first += [pltpu.VMEM((8, NZ, 512), F32), pltpu.VMEM((2, 9, 8, LANES), F32), pltpu.VMEM((9, 8, LANES), F32), pltpu.SemaphoreType.DMA((24,))]
    return first + [pltpu.SemaphoreType.DMA((N_SEMS,)), pltpu.SemaphoreType.DMA((N_SEMS,))]


def on_device(right_side, diffusivity, reaction):
    return pl.pallas_call(
        kernel,
        out_shape=jax.ShapeDtypeStruct((NZ, 8, 512), F32),
        in_specs=[pl.BlockSpec(memory_space=pl.ANY)] * 3,
        out_specs=pl.BlockSpec(memory_space=pl.ANY),
        scratch_shapes=shapes(),
        compiler_params=pltpu.CompilerParams(collective_id=0, has_side_effects=True, vmem_limit_bytes=VMEM_BYTES),
    )(right_side, diffusivity, reaction)


def solution(mesh):
    specs = P(None, "span", "width")
    return jax.shard_map(on_device, mesh=mesh, in_specs=(specs,) * 3, out_specs=specs, check_vma=False)
```

```python
import jax
import jax.numpy as jnp
from jax import lax
from jax.experimental import pallas as pl
from jax.experimental.pallas import tpu as pltpu
from jax.sharding import PartitionSpec as P


MESH = pl.DeviceIdType.MESH
F32 = jnp.float32
WEIGHT = 0.8
NZ = 32
LANES = 128
SPAN = 64
WIDTH = 8
ROWS = (12, 8, 6, 12, 6, 9)
TILES = (6, 3, 2, 1, 1, 1)
GRID_ROWS = (512, 256, 128, 64, 32, 16)
N_SEMS = 96
VMEM_BYTES = 62 << 20


class Level:
    def __init__(self, index, refs, base, width_at):
        self.index, self.base, self.width_at = index, base, width_at
        self.tiles = TILES[index]
        self.conduct, self.binding, self.source, self.smooth, self.fx, self.fy, self.fz, self.weight, self.work = refs
        self.scale = 0.25**index

    def cut(self, row):
        at = lax.rem(self.base + (row + 1 + GRID_ROWS[self.index]), GRID_ROWS[self.index])
        return jnp.where(at == 0, 0.0, 2.0 * self.scale).astype(F32)

    def y_factor(self, tile):
        halo, own = LANES >> self.index, 512 >> self.index
        low, high = halo - 1, halo + own - 1
        full = jnp.full((NZ, LANES), 2.0 * self.scale, F32)
        lane = lax.broadcasted_iota(jnp.int32, (NZ, LANES), 1)
        for place, edge in ((low, 0), (high, WIDTH - 1)):
            if place // LANES == tile:
                spot = jnp.where(self.width_at == edge, place % LANES, -1)
                full = jnp.where(lane == spot, 0.0, full)
        return full

    def y_factors(self):
        return [self.y_factor(tile) for tile in range(self.tiles)]

    def z_factor(self):
        depth = lax.broadcasted_iota(jnp.int32, (NZ, LANES), 0)
        return jnp.where(depth == NZ - 1, 0.0, 2.0 * self.scale)


def tile_of(ref, row, tile):
    return ref[row, :, pl.ds(tile * LANES, LANES)]


def put(ref, row, tile, value):
    ref[row, :, pl.ds(tile * LANES, LANES)] = value


def for_rows(first, last, body, unrolled):
    if unrolled:
        for row in range(first, last):
            body(row)
    else:
        lax.fori_loop(first, last, lambda row, carry: (body(row), carry)[1], 0, unroll=2 if (last - first) % 2 == 0 else 1)


def lane_above(tiles, tile):
    here = tiles[tile]
    after = tiles[min(tile + 1, len(tiles) - 1)]
    lane = lax.broadcasted_iota(jnp.int32, here.shape, 1)
    return pltpu.roll(jnp.where(lane == 0, after, here), LANES - 1, 1)


def lane_below(tiles, tile):
    here = tiles[tile]
    before = tiles[max(tile - 1, 0)]
    lane = lax.broadcasted_iota(jnp.int32, here.shape, 1)
    return pltpu.roll(jnp.where(lane == LANES - 1, before, here), 1, 1)


def depth_above(value):
    return pltpu.roll(value, NZ - 1, 0)


def depth_below(value):
    return pltpu.roll(value, 1, 0)


def mean_face(factor, first, second):
    return factor * (first * second) / (first + second)


def face_x(level, row, tiles):
    factor = level.cut(row)
    for tile in tiles:
        put(level.fx, row, tile, mean_face(factor, tile_of(level.conduct, row, tile), tile_of(level.conduct, row + 1, tile)))


def face_y(level, row, tiles, factors):
    for tile in tiles:
        near = {t: tile_of(level.conduct, row, t) for t in {tile, min(tile + 1, level.tiles - 1)}}
        after = near[min(tile + 1, level.tiles - 1)]
        put(level.fy, row, tile, mean_face(factors[tile], near[tile], lane_above((near[tile], after), 0)))


def face_z(level, row, tiles, factor):
    for tile in tiles:
        here = tile_of(level.conduct, row, tile)
        put(level.fz, row, tile, mean_face(factor, here, depth_above(here)))


def weigh(level, row, tiles):
    for tile in tiles:
        beside, deep = tile_of(level.fy, row, tile), tile_of(level.fz, row, tile)
        before = tile_of(level.fy, row, max(tile - 1, 0))
        diagonal = tile_of(level.fx, row - 1, tile) + tile_of(level.fx, row, tile)
        diagonal = diagonal + lane_below((before, beside), 1) + beside
        diagonal = diagonal + depth_below(deep) + deep + level.scale * tile_of(level.binding, row, tile)
        put(level.weight, row, tile, WEIGHT / diagonal)


def faces(level, first, last, unrolled):
    tiles = range(level.tiles)
    factors, deep_factor = level.y_factors(), level.z_factor()

    def one(row):
        face_x(level, row, tiles)
        face_y(level, row, tiles, factors)
        face_z(level, row, tiles, deep_factor)
        weigh(level, row, tiles)

    face_x(level, first - 1, tiles)
    for_rows(first, last, one, unrolled)


def smooth(level, first, last, unrolled):
    def one(row):
        for tile in range(level.tiles):
            put(level.smooth, row, tile, tile_of(level.weight, row, tile) * tile_of(level.source, row, tile))

    for_rows(first, last, one, unrolled)


def residual(level, field, row, wanted=None):
    wanted = wanted or range(level.tiles)
    cells = [tile_of(field, row, tile) for tile in range(level.tiles)]
    along = {
        tile: tile_of(level.fy, row, tile) * (lane_above(cells, tile) - cells[tile])
        for tile in range(max(wanted[0] - 1, 0), wanted[-1] + 1)
    }
    out = []
    for tile in wanted:
        here = cells[tile]
        deep = tile_of(level.fz, row, tile) * (depth_above(here) - here)
        value = tile_of(level.source, row, tile) - level.scale * tile_of(level.binding, row, tile) * here
        value = value + tile_of(level.fx, row, tile) * (tile_of(field, row + 1, tile) - here)
        value = value - tile_of(level.fx, row - 1, tile) * (here - tile_of(field, row - 1, tile))
        value = value + (along[tile] - lane_below(along, tile)) + (deep - depth_below(deep))
        out.append(value)
    return out


def relax(level, field, first, last, store, unrolled, wanted=None):
    def one(row):
        wanted_tiles = wanted or range(level.tiles)
        for tile, rest in zip(wanted_tiles, residual(level, field, row, wanted)):
            store(row, tile, tile_of(field, row, tile) + tile_of(level.weight, row, tile) * rest)

    for_rows(first, last, one, unrolled)


def exact_dot(value, selector):
    high = value.astype(jnp.bfloat16)
    left = value - high.astype(F32)
    middle = left.astype(jnp.bfloat16)
    low = (left - middle.astype(F32)).astype(jnp.bfloat16)
    total = jnp.dot(low, selector, preferred_element_type=F32) + jnp.dot(middle, selector, preferred_element_type=F32)
    return total + jnp.dot(high, selector, preferred_element_type=F32)


def coarsen(tiles_in, coarse_tiles, select):
    out = []
    for tile in range(coarse_tiles):
        if 2 * tile + 1 < len(tiles_in):
            pair = jnp.concatenate([tiles_in[2 * tile], tiles_in[2 * tile + 1]], axis=1)
            out.append(exact_dot(pair, select[0]))
        else:
            out.append(exact_dot(tiles_in[2 * tile], select[1]))
    return out


def kernel(right_ref, conduct_ref, binding_ref, out_ref, *scratch):
    levels_refs, (staged, packed_fields, packed_source, local_sem, coarse_send, coarse_recv) = scratch[:-6], scratch[-6:]
    span_at, width_at = lax.axis_index("span"), lax.axis_index("width")
    plane, across = span_at // 4, lax.rem(span_at, 4)
    d0, sb0, db1, s1, db2, s2, db3, s3, db5, s5 = levels_refs[:10]
    rest = list(levels_refs[10:])

    def take():
        return rest.pop(0)

    base = (8 * span_at - 2, 4 * span_at - 2, 2 * span_at - 2, 4 * plane - 4, 2 * plane - 2, plane - 4)
    d4, b4, s4 = take(), take(), take()
    own = [
        (d0, sb0.at[1], sb0.at[0]),
        (db1.at[0], db1.at[1], s1),
        (db2.at[0], db2.at[1], s2),
        (db3.at[0], db3.at[1], s3),
        (d4, b4, s4),
        (db5.at[0], db5.at[1], s5),
    ]
    levels = [Level(i, own[i] + tuple(take() for _ in range(6)), base[i], width_at) for i in range(6)]
    sums = take()
    lifts = take()
    iterates = [take() for _ in range(6)]

    def device(across_span, across_width=0):
        return (lax.rem(span_at + (across_span + SPAN), SPAN), lax.rem(width_at + (across_width + WIDTH), WIDTH))

    ring = [(1, 2), (-1, 2), (1, 1), (-1, 1), (1, 3), (-1, 3), (0, 2), (1, 0), (-1, 0), (0, 1), (0, 3)]

    def ring_device(dz, dx):
        to = lax.rem(across + dx, 4)
        return (lax.rem(4 * plane + (4 * dz + SPAN) + to, SPAN), width_at)

    around = [(1, 0), (-1, 0), (0, 1), (0, -1), (1, 1), (1, -1), (-1, 1), (-1, -1)]
    far = [(dz, 0) for dz in (2, -2, 3, -3, 4, -4)]

    barrier = pltpu.get_barrier_semaphore()
    partners = [device(a, b) for a, b in around if b != 0]
    partners += [ring_device(dz, dx) for dz, dx in ring] + [device(4 * dz) for dz, _ in far]
    for partner in partners:
        pl.semaphore_signal(barrier, inc=1, device_id=partner, device_id_type=MESH)

    inner = pl.ds(LANES, 4 * LANES)
    loads = []
    for i, (ref, target) in enumerate(((conduct_ref, d0), (binding_ref, sb0.at[1]), (right_ref, sb0.at[0]))):
        for row in range(8):
            loads.append(pltpu.make_async_copy(ref.at[:, row, :], target.at[2 + row, :, inner], local_sem.at[8 * i + row]))
            loads[-1].start()

    lane = lax.broadcasted_iota(jnp.int32, (2 * LANES, LANES), 0) // 2
    column = lax.broadcasted_iota(jnp.int32, (2 * LANES, LANES), 1)
    pair_select = jnp.where(lane == column, 0.25, 0.0).astype(jnp.bfloat16)
    lane = lax.broadcasted_iota(jnp.int32, (LANES, LANES), 0) // 2
    column = lax.broadcasted_iota(jnp.int32, (LANES, LANES), 1)
    twice_select = jnp.where(lane == lax.rem(column, LANES // 2), 0.25, 0.0).astype(jnp.bfloat16)
    select = (pair_select, twice_select)
    lane = lax.broadcasted_iota(jnp.int32, (LANES, LANES), 0)
    column = lax.broadcasted_iota(jnp.int32, (LANES, LANES), 1) // 2
    spread = tuple(jnp.where(lane == column + half * (LANES // 2), 1.0, 0.0).astype(jnp.bfloat16) for half in (0, 1))

    pl.semaphore_wait(barrier, len(partners))

    copies = []

    def send(source, target, to):
        at = len(copies)
        copy = pltpu.make_async_remote_copy(
            src_ref=source, dst_ref=target, send_sem=coarse_send.at[at], recv_sem=coarse_recv.at[at], device_id=to, device_id_type=MESH
        )
        copy.start()
        copies.append(copy)
        return copy

    def arrive(group):
        for copy in group:
            copy.wait_recv()

    for load in loads[:8]:
        load.wait()
    rows_d = [send(d0.at[pl.ds(8, 2), :, inner], d0.at[pl.ds(0, 2), :, inner], device(1)), send(d0.at[pl.ds(2, 2), :, inner], d0.at[pl.ds(10, 2), :, inner], device(-1))]
    def sideways(source, spans):
        sent = []
        for b in (1, -1):
            lanes_from, lanes_to = (pl.ds(4 * LANES, LANES), pl.ds(0, LANES)) if b == 1 else (pl.ds(LANES, LANES), pl.ds(5 * LANES, LANES))
            for a, rows_from, rows_to in spans:
                sent.append(send(source.at[rows_from, :, lanes_from], source.at[rows_to, :, lanes_to], device(a, b)))
        return sent

    beside = ((0, pl.ds(2, 8), pl.ds(2, 8)),)
    corner = ((1, pl.ds(9, 1), pl.ds(1, 1)), (-1, pl.ds(2, 1), pl.ds(10, 1)))
    lanes_d = sideways(d0, beside)
    corners_d = sideways(d0, ((1, pl.ds(8, 2), pl.ds(0, 2)), (-1, pl.ds(2, 2), pl.ds(10, 2))))
    for load in loads[8:16]:
        load.wait()
    rows_b = [send(sb0.at[1, pl.ds(9, 1), :, inner], sb0.at[1, pl.ds(1, 1), :, inner], device(1)), send(sb0.at[1, pl.ds(2, 1), :, inner], sb0.at[1, pl.ds(10, 1), :, inner], device(-1))]
    lanes_b = sideways(sb0.at[1], beside)
    corners_b = sideways(sb0.at[1], corner)
    for load in loads[16:]:
        load.wait()
    rows_s = [send(sb0.at[0, pl.ds(9, 1), :, inner], sb0.at[0, pl.ds(1, 1), :, inner], device(1)), send(sb0.at[0, pl.ds(2, 1), :, inner], sb0.at[0, pl.ds(10, 1), :, inner], device(-1))]
    lanes_s = sideways(sb0.at[0], beside)
    corners_s = sideways(sb0.at[0], corner)

    l0, l1, l2, l3, l4, l5 = levels
    factors_0, deep_0 = l0.y_factors(), l0.z_factor()

    def inside(row):
        face_x(l0, row, range(1, 5))
        face_y(l0, row, range(1, 4), factors_0)
        face_z(l0, row, range(1, 5), deep_0)

        @pl.when(row > 2)
        def _():
            weigh(l0, row, (2, 3))

    for_rows(2, 9, inside, False)
    face_y(l0, 9, range(1, 4), factors_0)
    face_z(l0, 9, range(1, 5), deep_0)

    arrive(rows_d)
    for row in (0, 1, 9, 10):
        face_x(l0, row, range(1, 5))
    for row in (1, 10):
        face_y(l0, row, range(1, 4), factors_0)
        face_z(l0, row, range(1, 5), deep_0)
    for row in (2, 9):
        weigh(l0, row, (2, 3))
    arrive(lanes_d)

    def outside(row):
        face_y(l0, row, (0, 4, 5), factors_0)
        face_z(l0, row, (0, 5), deep_0)

    def outside_x(row):
        outside(row)
        face_x(l0, row, (0, 5))

    for_rows(3, 9, outside_x, False)
    outside_x(2)
    outside(9)
    arrive(lanes_b)
    for_rows(3, 9, lambda row: weigh(l0, row, (0, 1, 4, 5)), False)
    for row in (2, 9):
        weigh(l0, row, (1, 4))
    arrive(rows_b)
    for row in (1, 10):
        weigh(l0, row, (2, 3))
    arrive(corners_d)
    for row in (0, 1, 9, 10):
        face_x(l0, row, (0, 5))
    for row in (1, 10):
        face_y(l0, row, (0, 4, 5), factors_0)
        face_z(l0, row, (0, 5), deep_0)
    arrive(corners_b)
    for row in (2, 9):
        weigh(l0, row, (0, 5))
    for row in (1, 10):
        weigh(l0, row, (0, 1, 4, 5))

    def coarse_field(fine, coarse, n_rows, fine_row, coarse_row):
        tiles = [
            jnp.concatenate([tile_of(fine[0], fine_row + 2 * i, t) + tile_of(fine[0], fine_row + 2 * i + 1, t) for i in range(n_rows)], axis=0)
            for t in range(fine[1])
        ]
        for t, value in enumerate(coarsen(tiles, coarse[1], select)):
            for i in range(n_rows):
                put(coarse[0], coarse_row + i, t, value[i * NZ : (i + 1) * NZ])

    def coarse_conduct(fine, coarse, n_rows, fine_row, coarse_row):
        coarse_field((fine.conduct, fine.tiles), (coarse.conduct, coarse.tiles), n_rows, fine_row, coarse_row)

    def coarse_binding(fine, coarse, n_rows, fine_row, coarse_row):
        coarse_field((fine.binding, fine.tiles), (coarse.binding, coarse.tiles), n_rows, fine_row, coarse_row)

    def coarse_fields(fine, coarse, n_rows, fine_row, coarse_row):
        coarse_conduct(fine, coarse, n_rows, fine_row, coarse_row)
        coarse_binding(fine, coarse, n_rows, fine_row, coarse_row)

    def coarse_source(fine, coarse, n_rows, fine_row, coarse_row, unrolled):
        def one(i):
            low = residual(fine, fine.smooth, fine_row + 2 * i)
            high = residual(fine, fine.smooth, fine_row + 2 * i + 1)
            for t in range(fine.tiles):
                put(sums, i, t, low[t] + high[t])

        for_rows(0, n_rows, one, unrolled)
        tiles = [jnp.concatenate([tile_of(sums, i, t) for i in range(n_rows)], axis=0) for t in range(fine.tiles)]
        for t, value in enumerate(coarsen(tiles, coarse.tiles, select)):
            for i in range(n_rows):
                put(coarse.source, coarse_row + i, t, value[i * NZ : (i + 1) * NZ])

    def pack(value):
        lane = lax.broadcasted_iota(jnp.int32, (8, LANES), 1) // 32
        out = value[0:8]
        for group in range(1, 4):
            out = jnp.where(lane == group, pltpu.roll(value[8 * group : 8 * group + 8], 32 * group, 1), out)
        return out

    def unpack(value):
        return jnp.concatenate([value] + [pltpu.roll(value, LANES - 32 * group, 1) for group in range(1, 4)], axis=0)

    coarse_conduct(l0, l1, 6, 0, 1)
    coarse_binding(l0, l1, 4, 2, 2)
    fields_1 = []
    for to, d_from, d_to, b_from, b_to in ((1, 4, 0, 5, 1), (-1, 3, 7, 2, 6)):
        fields_1.append(send(db1.at[0, pl.ds(d_from, 1)], db1.at[0, pl.ds(d_to, 1)], device(to)))
        fields_1.append(send(db1.at[1, pl.ds(b_from, 1)], db1.at[1, pl.ds(b_to, 1)], device(to)))

    arrive(rows_s + lanes_s + corners_s)
    smooth(l0, 1, 11, False)
    coarse_source(l0, l1, 4, 2, 2, False)

    sources_1 = [send(s1.at[pl.ds(5, 1)], s1.at[pl.ds(1, 1)], device(1)), send(s1.at[pl.ds(2, 1)], s1.at[pl.ds(6, 1)], device(-1))]

    coarse_fields(l1, l2, 2, 2, 2)
    fields_2 = []
    for to, d_from, d_to, b_from, b_to in ((1, 2, 0, 3, 1), (-1, 3, 5, 2, 4)):
        fields_2.append(send(db2.at[0, pl.ds(d_from, 1)], db2.at[0, pl.ds(d_to, 1)], device(to)))
        fields_2.append(send(db2.at[1, pl.ds(b_from, 1)], db2.at[1, pl.ds(b_to, 1)], device(to)))
    factors_1, deep_1 = l1.y_factors(), l1.z_factor()
    for row in (2, 3, 4, 5):
        face_y(l1, row, range(3), factors_1)
        face_z(l1, row, range(3), deep_1)
    for row in (1, 2, 3, 4, 5):
        face_x(l1, row, range(3))
    for row in (1, 6):
        face_y(l1, row, range(3), factors_1)
        face_z(l1, row, range(3), deep_1)
    for row in (3, 4):
        weigh(l1, row, range(3))
    mine = 4 + across
    coarse_fields(l2, l3, 1, 2, mine)
    arrive(fields_1)
    for row in (0, 6):
        face_x(l1, row, range(3))
    for row in (1, 2, 5, 6):
        weigh(l1, row, range(3))
    coarse_conduct(l1, l2, 1, 0, 1)
    coarse_conduct(l1, l2, 1, 6, 4)
    arrive(sources_1)
    smooth(l1, 1, 7, True)
    coarse_source(l1, l2, 2, 2, 2, True)

    sources_2 = [send(s2.at[pl.ds(3, 1)], s2.at[pl.ds(1, 1)], device(1)), send(s2.at[pl.ds(2, 1)], s2.at[pl.ds(4, 1)], device(-1))]
    smooths_1 = [send(l1.smooth.at[pl.ds(4, 1)], l1.smooth.at[pl.ds(0, 1)], device(1)), send(l1.smooth.at[pl.ds(3, 1)], l1.smooth.at[pl.ds(7, 1)], device(-1))]
    fields_3 = [
        send(db3.at[:, pl.ds(mine, 1)], db3.at[:, pl.ds(4 * (1 - dz) + across, 1)], ring_device(dz, dx)) for dz, dx in ring
    ]
    arrive(fields_2)
    faces(l2, 1, 5, True)
    arrive(sources_2)
    smooth(l2, 1, 5, True)
    coarse_source(l2, l3, 1, 2, mine, True)

    sources_3 = [
        send(s3.at[pl.ds(mine, 1)], s3.at[pl.ds(4 * (1 - dz) + across, 1)], ring_device(dz, dx)) for dz, dx in ring
    ]
    smooths_2 = [send(l2.smooth.at[pl.ds(2, 1)], l2.smooth.at[pl.ds(0, 1)], device(1)), send(l2.smooth.at[pl.ds(3, 1)], l2.smooth.at[pl.ds(5, 1)], device(-1))]
    arrive(fields_3)
    coarse_fields(l3, l4, 6, 0, 0)
    coarse_fields(l4, l5, 1, 2, 4)
    for i in range(2):
        packed_fields[i, 4] = pack(db5[i, 4])
    fields_5 = [
        send(packed_fields.at[:, pl.ds(4, 1)], packed_fields.at[:, pl.ds(4 - dz, 1)], device(4 * dz)) for dz in (4, -4, 3, -3, 2, -2, 1, -1)
    ]
    faces(l3, 1, 11, False)
    faces(l4, 1, 5, True)
    arrive(sources_3)
    smooth(l3, 1, 11, True)
    coarse_source(l3, l4, 4, 2, 1, True)
    smooth(l4, 1, 5, True)
    coarse_source(l4, l5, 1, 2, 4, True)

    packed_source[4] = pack(s5[4])
    sources_5 = [send(packed_source.at[pl.ds(4, 1)], packed_source.at[pl.ds(4 - dz, 1)], device(4 * dz)) for dz in (3, -3, 2, -2, 1, -1)]
    smooths_4 = [send(l4.smooth.at[pl.ds(2, 1)], l4.smooth.at[pl.ds(0, 1)], device(4)), send(l4.smooth.at[pl.ds(3, 1)], l4.smooth.at[pl.ds(5, 1)], device(-4))]
    arrive(fields_5)
    for row in (0, 1, 2, 3, 5, 6, 7, 8):
        for i in range(2):
            db5[i, row] = unpack(packed_fields[i, row])
    faces(l5, 1, 8, True)
    arrive(sources_5)
    for row in (1, 2, 3, 5, 6, 7):
        s5[row] = unpack(packed_source[row])

    smooth(l5, 1, 8, True)

    def into(ref):
        return lambda row, tile, value: put(ref, row, tile, value)

    relax(l5, l5.smooth, 2, 7, into(l5.work), True)
    relax(l5, l5.work, 3, 6, into(iterates[5]), True)

    def lift(fine, coarse_ref, coarse_rows, coarse_tiles, first_row, last_row, coarse_of):
        values = [jnp.concatenate([tile_of(coarse_ref, c, t) for c in coarse_rows], axis=0) for t in range(coarse_tiles)]
        for t in range(fine.tiles):
            spread_out = exact_dot(values[t // 2], spread[t % 2])
            for row in range(first_row, last_row):
                at = coarse_of(row)
                put(lifts, row, t, tile_of(fine.smooth, row, t) + spread_out[at * NZ : (at + 1) * NZ])

    arrive(smooths_4)
    lift(l4, iterates[5], range(3, 6), 1, 0, 6, lambda row: row // 2)
    relax(l4, lifts, 1, 5, into(iterates[4]), True)
    lift(l3, iterates[4], range(1, 5), 1, 2, 10, lambda row: row // 2 - 1)
    relax(l3, lifts, 3, 9, into(iterates[3]), True)
    arrive(smooths_2)
    lift(l2, iterates[3], [across + 3 + i for i in range(3)], 1, 0, 6, lambda row: row // 2)
    relax(l2, lifts, 1, 5, into(iterates[2]), True)
    arrive(smooths_1)
    lift(l1, iterates[2], range(1, 5), 2, 0, 8, lambda row: row // 2)
    relax(l1, lifts, 1, 7, into(iterates[1]), True)
    lift(l0, iterates[1], range(1, 7), 3, 1, 11, lambda row: (row - 2) // 2 + 1)

    stores = []

    def finish(row, tile, value):
        put(staged, row - 2, tile - 1, value)
        if tile == 4:
            stores.append(pltpu.make_async_copy(staged.at[row - 2], out_ref.at[:, row - 2, :], local_sem.at[row - 2]))
            stores[-1].start()

    relax(l0, lifts, 2, 10, finish, True, range(1, 5))
    for copy in stores:
        copy.wait()
    for copy in copies:
        copy.wait_send()


def shapes():
    def rows(level, *lead):
        return pltpu.VMEM((*lead, ROWS[level], NZ, TILES[level] * LANES), F32)

    first = [rows(0), rows(0, 2), rows(1, 2), rows(1), rows(2, 2), rows(2), rows(3, 2), rows(3), rows(5, 2), rows(5)]
    first += [rows(4), rows(4), rows(4)]
    for level in range(6):
        first += [rows(level) for _ in range(6)]
    first += [pltpu.VMEM((4, NZ, TILES[0] * LANES), F32), pltpu.VMEM((12, NZ, TILES[0] * LANES), F32)]
    first += [rows(level) for level in range(6)]
    first += [pltpu.VMEM((8, NZ, 512), F32), pltpu.VMEM((2, 9, 8, LANES), F32), pltpu.VMEM((9, 8, LANES), F32), pltpu.SemaphoreType.DMA((24,))]
    return first + [pltpu.SemaphoreType.DMA((N_SEMS,)), pltpu.SemaphoreType.DMA((N_SEMS,))]


def on_device(right_side, diffusivity, reaction):
    return pl.pallas_call(
        kernel,
        out_shape=jax.ShapeDtypeStruct((NZ, 8, 512), F32),
        in_specs=[pl.BlockSpec(memory_space=pl.ANY)] * 3,
        out_specs=pl.BlockSpec(memory_space=pl.ANY),
        scratch_shapes=shapes(),
        compiler_params=pltpu.CompilerParams(collective_id=0, has_side_effects=True, vmem_limit_bytes=VMEM_BYTES),
    )(right_side, diffusivity, reaction)


def solution(mesh):
    specs = P(None, "span", "width")
    return jax.shard_map(on_device, mesh=mesh, in_specs=(specs,) * 3, out_specs=specs, check_vma=False)
```

```python
import jax
import jax.numpy as jnp
from jax import lax
from jax.experimental import pallas as pl
from jax.experimental.pallas import tpu as pltpu
from jax.sharding import PartitionSpec as P


MESH = pl.DeviceIdType.MESH
F32 = jnp.float32
WEIGHT = 0.8
NZ = 32
LANES = 128
SPAN = 64
WIDTH = 8
ROWS = (12, 8, 6, 12, 6, 9)
TILES = (6, 3, 2, 1, 1, 1)
GRID_ROWS = (512, 256, 128, 64, 32, 16)
N_SEMS = 96
VMEM_BYTES = 62 << 20


class Level:
    def __init__(self, index, refs, base, width_at):
        self.index, self.base, self.width_at = index, base, width_at
        self.tiles = TILES[index]
        self.conduct, self.binding, self.source, self.smooth, self.fx, self.fy, self.fz, self.weight, self.work = refs
        self.scale = 0.25**index

    def cut(self, row):
        at = lax.rem(self.base + (row + 1 + GRID_ROWS[self.index]), GRID_ROWS[self.index])
        return jnp.where(at == 0, 0.0, 2.0 * self.scale).astype(F32)

    def y_factor(self, tile):
        halo, own = LANES >> self.index, 512 >> self.index
        low, high = halo - 1, halo + own - 1
        full = jnp.full((NZ, LANES), 2.0 * self.scale, F32)
        lane = lax.broadcasted_iota(jnp.int32, (NZ, LANES), 1)
        for place, edge in ((low, 0), (high, WIDTH - 1)):
            if place // LANES == tile:
                spot = jnp.where(self.width_at == edge, place % LANES, -1)
                full = jnp.where(lane == spot, 0.0, full)
        return full

    def y_factors(self):
        return [self.y_factor(tile) for tile in range(self.tiles)]

    def z_factor(self):
        depth = lax.broadcasted_iota(jnp.int32, (NZ, LANES), 0)
        return jnp.where(depth == NZ - 1, 0.0, 2.0 * self.scale)


def tile_of(ref, row, tile):
    return ref[row, :, pl.ds(tile * LANES, LANES)]


def put(ref, row, tile, value):
    ref[row, :, pl.ds(tile * LANES, LANES)] = value


def for_rows(first, last, body, unrolled):
    if unrolled:
        for row in range(first, last):
            body(row)
    else:
        lax.fori_loop(first, last, lambda row, carry: (body(row), carry)[1], 0, unroll=2 if (last - first) % 2 == 0 else 1)


def lane_above(tiles, tile):
    here = tiles[tile]
    after = tiles[min(tile + 1, len(tiles) - 1)]
    lane = lax.broadcasted_iota(jnp.int32, here.shape, 1)
    return pltpu.roll(jnp.where(lane == 0, after, here), LANES - 1, 1)


def lane_below(tiles, tile):
    here = tiles[tile]
    before = tiles[max(tile - 1, 0)]
    lane = lax.broadcasted_iota(jnp.int32, here.shape, 1)
    return pltpu.roll(jnp.where(lane == LANES - 1, before, here), 1, 1)


def depth_above(value):
    return pltpu.roll(value, NZ - 1, 0)


def depth_below(value):
    return pltpu.roll(value, 1, 0)


def mean_face(factor, first, second):
    return factor * (first * second) / (first + second)


def face_x(level, row, tiles):
    factor = level.cut(row)
    for tile in tiles:
        put(level.fx, row, tile, mean_face(factor, tile_of(level.conduct, row, tile), tile_of(level.conduct, row + 1, tile)))


def face_y(level, row, tiles, factors):
    for tile in tiles:
        near = {t: tile_of(level.conduct, row, t) for t in {tile, min(tile + 1, level.tiles - 1)}}
        after = near[min(tile + 1, level.tiles - 1)]
        put(level.fy, row, tile, mean_face(factors[tile], near[tile], lane_above((near[tile], after), 0)))


def face_z(level, row, tiles, factor):
    for tile in tiles:
        here = tile_of(level.conduct, row, tile)
        put(level.fz, row, tile, mean_face(factor, here, depth_above(here)))


def weigh(level, row, tiles):
    for tile in tiles:
        beside, deep = tile_of(level.fy, row, tile), tile_of(level.fz, row, tile)
        before = tile_of(level.fy, row, max(tile - 1, 0))
        diagonal = tile_of(level.fx, row - 1, tile) + tile_of(level.fx, row, tile)
        diagonal = diagonal + lane_below((before, beside), 1) + beside
        diagonal = diagonal + depth_below(deep) + deep + level.scale * tile_of(level.binding, row, tile)
        put(level.weight, row, tile, WEIGHT / diagonal)


def faces(level, first, last, unrolled):
    tiles = range(level.tiles)
    factors, deep_factor = level.y_factors(), level.z_factor()

    def one(row):
        face_x(level, row, tiles)
        face_y(level, row, tiles, factors)
        face_z(level, row, tiles, deep_factor)
        weigh(level, row, tiles)

    face_x(level, first - 1, tiles)
    for_rows(first, last, one, unrolled)


def smooth(level, first, last, unrolled):
    def one(row):
        for tile in range(level.tiles):
            put(level.smooth, row, tile, tile_of(level.weight, row, tile) * tile_of(level.source, row, tile))

    for_rows(first, last, one, unrolled)


def residual(level, field, row, wanted=None):
    wanted = wanted or range(level.tiles)
    cells = [tile_of(field, row, tile) for tile in range(level.tiles)]
    along = {
        tile: tile_of(level.fy, row, tile) * (lane_above(cells, tile) - cells[tile])
        for tile in range(max(wanted[0] - 1, 0), wanted[-1] + 1)
    }
    out = []
    for tile in wanted:
        here = cells[tile]
        deep = tile_of(level.fz, row, tile) * (depth_above(here) - here)
        value = tile_of(level.source, row, tile) - level.scale * tile_of(level.binding, row, tile) * here
        value = value + tile_of(level.fx, row, tile) * (tile_of(field, row + 1, tile) - here)
        value = value - tile_of(level.fx, row - 1, tile) * (here - tile_of(field, row - 1, tile))
        value = value + (along[tile] - lane_below(along, tile)) + (deep - depth_below(deep))
        out.append(value)
    return out


def relax(level, field, first, last, store, unrolled, wanted=None):
    def one(row):
        wanted_tiles = wanted or range(level.tiles)
        for tile, rest in zip(wanted_tiles, residual(level, field, row, wanted)):
            store(row, tile, tile_of(field, row, tile) + tile_of(level.weight, row, tile) * rest)

    for_rows(first, last, one, unrolled)


def exact_dot(value, selector):
    high = value.astype(jnp.bfloat16)
    left = value - high.astype(F32)
    middle = left.astype(jnp.bfloat16)
    low = (left - middle.astype(F32)).astype(jnp.bfloat16)
    total = jnp.dot(low, selector, preferred_element_type=F32) + jnp.dot(middle, selector, preferred_element_type=F32)
    return total + jnp.dot(high, selector, preferred_element_type=F32)


def coarsen(tiles_in, coarse_tiles, select):
    out = []
    for tile in range(coarse_tiles):
        if 2 * tile + 1 < len(tiles_in):
            pair = jnp.concatenate([tiles_in[2 * tile], tiles_in[2 * tile + 1]], axis=1)
            out.append(exact_dot(pair, select[0]))
        else:
            out.append(exact_dot(tiles_in[2 * tile], select[1]))
    return out


def kernel(right_ref, conduct_ref, binding_ref, out_ref, *scratch):
    levels_refs, (staged, packed_fields, packed_source, local_sem, coarse_send, coarse_recv) = scratch[:-6], scratch[-6:]
    span_at, width_at = lax.axis_index("span"), lax.axis_index("width")
    plane, across = span_at // 4, lax.rem(span_at, 4)
    d0, sb0, db1, s1, db2, s2, db3, s3, db5, s5 = levels_refs[:10]
    rest = list(levels_refs[10:])

    def take():
        return rest.pop(0)

    base = (8 * span_at - 2, 4 * span_at - 2, 2 * span_at - 2, 4 * plane - 4, 2 * plane - 2, plane - 4)
    d4, b4, s4 = take(), take(), take()
    own = [
        (d0, sb0.at[1], sb0.at[0]),
        (db1.at[0], db1.at[1], s1),
        (db2.at[0], db2.at[1], s2),
        (db3.at[0], db3.at[1], s3),
        (d4, b4, s4),
        (db5.at[0], db5.at[1], s5),
    ]
    levels = [Level(i, own[i] + tuple(take() for _ in range(6)), base[i], width_at) for i in range(6)]
    sums = take()
    lifts = take()
    iterates = [take() for _ in range(6)]

    def device(across_span, across_width=0):
        return (lax.rem(span_at + (across_span + SPAN), SPAN), lax.rem(width_at + (across_width + WIDTH), WIDTH))

    ring = [(1, 2), (-1, 2), (1, 1), (-1, 1), (1, 3), (-1, 3), (0, 2), (1, 0), (-1, 0), (0, 1), (0, 3)]

    def ring_device(dz, dx):
        to = lax.rem(across + dx, 4)
        return (lax.rem(4 * plane + (4 * dz + SPAN) + to, SPAN), width_at)

    around = [(1, 0), (-1, 0), (0, 1), (0, -1), (1, 1), (1, -1), (-1, 1), (-1, -1)]
    far = [(dz, 0) for dz in (2, -2, 3, -3, 4, -4)]

    barrier = pltpu.get_barrier_semaphore()
    partners = [device(a, b) for a, b in around if b != 0]
    partners += [ring_device(dz, dx) for dz, dx in ring] + [device(4 * dz) for dz, _ in far]
    for partner in partners:
        pl.semaphore_signal(barrier, inc=1, device_id=partner, device_id_type=MESH)

    inner = pl.ds(LANES, 4 * LANES)
    loads = []
    for i, (ref, target) in enumerate(((conduct_ref, d0), (binding_ref, sb0.at[1]), (right_ref, sb0.at[0]))):
        for row in (0, 7, 1, 6, 2, 3, 4, 5):
            loads.append(pltpu.make_async_copy(ref.at[:, row, :], target.at[2 + row, :, inner], local_sem.at[8 * i + row]))
            loads[-1].start()

    lane = lax.broadcasted_iota(jnp.int32, (2 * LANES, LANES), 0) // 2
    column = lax.broadcasted_iota(jnp.int32, (2 * LANES, LANES), 1)
    pair_select = jnp.where(lane == column, 0.25, 0.0).astype(jnp.bfloat16)
    lane = lax.broadcasted_iota(jnp.int32, (LANES, LANES), 0) // 2
    column = lax.broadcasted_iota(jnp.int32, (LANES, LANES), 1)
    twice_select = jnp.where(lane == lax.rem(column, LANES // 2), 0.25, 0.0).astype(jnp.bfloat16)
    select = (pair_select, twice_select)
    lane = lax.broadcasted_iota(jnp.int32, (LANES, LANES), 0)
    column = lax.broadcasted_iota(jnp.int32, (LANES, LANES), 1) // 2
    spread = tuple(jnp.where(lane == column + half * (LANES // 2), 1.0, 0.0).astype(jnp.bfloat16) for half in (0, 1))

    pl.semaphore_wait(barrier, len(partners))

    copies = []

    def send(source, target, to):
        at = len(copies)
        copy = pltpu.make_async_remote_copy(
            src_ref=source, dst_ref=target, send_sem=coarse_send.at[at], recv_sem=coarse_recv.at[at], device_id=to, device_id_type=MESH
        )
        copy.start()
        copies.append(copy)
        return copy

    def arrive(group):
        for copy in group:
            copy.wait_recv()

    for load in loads[:4]:
        load.wait()
    rows_d = [send(d0.at[pl.ds(8, 2), :, inner], d0.at[pl.ds(0, 2), :, inner], device(1)), send(d0.at[pl.ds(2, 2), :, inner], d0.at[pl.ds(10, 2), :, inner], device(-1))]
    def sideways(source, spans):
        sent = []
        for b in (1, -1):
            lanes_from, lanes_to = (pl.ds(4 * LANES, LANES), pl.ds(0, LANES)) if b == 1 else (pl.ds(LANES, LANES), pl.ds(5 * LANES, LANES))
            for a, rows_from, rows_to in spans:
                sent.append(send(source.at[rows_from, :, lanes_from], source.at[rows_to, :, lanes_to], device(a, b)))
        return sent

    beside = ((0, pl.ds(2, 8), pl.ds(2, 8)),)
    corner = ((1, pl.ds(9, 1), pl.ds(1, 1)), (-1, pl.ds(2, 1), pl.ds(10, 1)))
    for load in loads[4:8]:
        load.wait()
    lanes_d = sideways(d0, beside)
    corners_d = sideways(d0, ((1, pl.ds(8, 2), pl.ds(0, 2)), (-1, pl.ds(2, 2), pl.ds(10, 2))))
    for load in loads[8:16]:
        load.wait()
    rows_b = [send(sb0.at[1, pl.ds(9, 1), :, inner], sb0.at[1, pl.ds(1, 1), :, inner], device(1)), send(sb0.at[1, pl.ds(2, 1), :, inner], sb0.at[1, pl.ds(10, 1), :, inner], device(-1))]
    lanes_b = sideways(sb0.at[1], beside)
    corners_b = sideways(sb0.at[1], corner)
    for load in loads[16:]:
        load.wait()
    rows_s = [send(sb0.at[0, pl.ds(9, 1), :, inner], sb0.at[0, pl.ds(1, 1), :, inner], device(1)), send(sb0.at[0, pl.ds(2, 1), :, inner], sb0.at[0, pl.ds(10, 1), :, inner], device(-1))]
    lanes_s = sideways(sb0.at[0], beside)
    corners_s = sideways(sb0.at[0], corner)

    l0, l1, l2, l3, l4, l5 = levels
    factors_0, deep_0 = l0.y_factors(), l0.z_factor()

    def inside(row):
        face_x(l0, row, range(1, 5))
        face_y(l0, row, range(1, 4), factors_0)
        face_z(l0, row, range(1, 5), deep_0)

        @pl.when(row > 2)
        def _():
            weigh(l0, row, (2, 3))

    for_rows(2, 9, inside, False)
    face_y(l0, 9, range(1, 4), factors_0)
    face_z(l0, 9, range(1, 5), deep_0)

    arrive(rows_d)
    for row in (0, 1, 9, 10):
        face_x(l0, row, range(1, 5))
    for row in (1, 10):
        face_y(l0, row, range(1, 4), factors_0)
        face_z(l0, row, range(1, 5), deep_0)
    for row in (2, 9):
        weigh(l0, row, (2, 3))
    arrive(lanes_d)

    def outside(row):
        face_y(l0, row, (0, 4, 5), factors_0)
        face_z(l0, row, (0, 5), deep_0)

    def outside_x(row):
        outside(row)
        face_x(l0, row, (0, 5))

    for_rows(3, 9, outside_x, False)
    outside_x(2)
    outside(9)
    arrive(lanes_b)
    for_rows(3, 9, lambda row: weigh(l0, row, (0, 1, 4, 5)), False)
    for row in (2, 9):
        weigh(l0, row, (1, 4))
    arrive(rows_b)
    for row in (1, 10):
        weigh(l0, row, (2, 3))
    arrive(corners_d)
    for row in (0, 1, 9, 10):
        face_x(l0, row, (0, 5))
    for row in (1, 10):
        face_y(l0, row, (0, 4, 5), factors_0)
        face_z(l0, row, (0, 5), deep_0)
    arrive(corners_b)
    for row in (2, 9):
        weigh(l0, row, (0, 5))
    for row in (1, 10):
        weigh(l0, row, (0, 1, 4, 5))

    def coarse_field(fine, coarse, n_rows, fine_row, coarse_row):
        tiles = [
            jnp.concatenate([tile_of(fine[0], fine_row + 2 * i, t) + tile_of(fine[0], fine_row + 2 * i + 1, t) for i in range(n_rows)], axis=0)
            for t in range(fine[1])
        ]
        for t, value in enumerate(coarsen(tiles, coarse[1], select)):
            for i in range(n_rows):
                put(coarse[0], coarse_row + i, t, value[i * NZ : (i + 1) * NZ])

    def coarse_conduct(fine, coarse, n_rows, fine_row, coarse_row):
        coarse_field((fine.conduct, fine.tiles), (coarse.conduct, coarse.tiles), n_rows, fine_row, coarse_row)

    def coarse_binding(fine, coarse, n_rows, fine_row, coarse_row):
        coarse_field((fine.binding, fine.tiles), (coarse.binding, coarse.tiles), n_rows, fine_row, coarse_row)

    def coarse_fields(fine, coarse, n_rows, fine_row, coarse_row):
        coarse_conduct(fine, coarse, n_rows, fine_row, coarse_row)
        coarse_binding(fine, coarse, n_rows, fine_row, coarse_row)

    def coarse_source(fine, coarse, n_rows, fine_row, coarse_row, unrolled):
        def one(i):
            low = residual(fine, fine.smooth, fine_row + 2 * i)
            high = residual(fine, fine.smooth, fine_row + 2 * i + 1)
            for t in range(fine.tiles):
                put(sums, i, t, low[t] + high[t])

        for_rows(0, n_rows, one, unrolled)
        tiles = [jnp.concatenate([tile_of(sums, i, t) for i in range(n_rows)], axis=0) for t in range(fine.tiles)]
        for t, value in enumerate(coarsen(tiles, coarse.tiles, select)):
            for i in range(n_rows):
                put(coarse.source, coarse_row + i, t, value[i * NZ : (i + 1) * NZ])

    def pack(value):
        lane = lax.broadcasted_iota(jnp.int32, (8, LANES), 1) // 32
        out = value[0:8]
        for group in range(1, 4):
            out = jnp.where(lane == group, pltpu.roll(value[8 * group : 8 * group + 8], 32 * group, 1), out)
        return out

    def unpack(value):
        return jnp.concatenate([value] + [pltpu.roll(value, LANES - 32 * group, 1) for group in range(1, 4)], axis=0)

    coarse_conduct(l0, l1, 6, 0, 1)
    coarse_binding(l0, l1, 4, 2, 2)
    fields_1 = []
    for to, d_from, d_to, b_from, b_to in ((1, 4, 0, 5, 1), (-1, 3, 7, 2, 6)):
        fields_1.append(send(db1.at[0, pl.ds(d_from, 1)], db1.at[0, pl.ds(d_to, 1)], device(to)))
        fields_1.append(send(db1.at[1, pl.ds(b_from, 1)], db1.at[1, pl.ds(b_to, 1)], device(to)))

    def smooth_tiles(row, tiles):
        for tile in tiles:
            put(l0.smooth, row, tile, tile_of(l0.weight, row, tile) * tile_of(l0.source, row, tile))

    for_rows(2, 10, lambda row: smooth_tiles(row, range(1, 5)), False)
    arrive(rows_s + lanes_s + corners_s)
    for_rows(2, 10, lambda row: smooth_tiles(row, (0, 5)), False)
    for row in (1, 10):
        smooth_tiles(row, range(6))
    coarse_source(l0, l1, 4, 2, 2, False)

    sources_1 = [send(s1.at[pl.ds(5, 1)], s1.at[pl.ds(1, 1)], device(1)), send(s1.at[pl.ds(2, 1)], s1.at[pl.ds(6, 1)], device(-1))]

    coarse_fields(l1, l2, 2, 2, 2)
    fields_2 = []
    for to, d_from, d_to, b_from, b_to in ((1, 2, 0, 3, 1), (-1, 3, 5, 2, 4)):
        fields_2.append(send(db2.at[0, pl.ds(d_from, 1)], db2.at[0, pl.ds(d_to, 1)], device(to)))
        fields_2.append(send(db2.at[1, pl.ds(b_from, 1)], db2.at[1, pl.ds(b_to, 1)], device(to)))
    factors_1, deep_1 = l1.y_factors(), l1.z_factor()
    for row in (2, 3, 4, 5):
        face_y(l1, row, range(3), factors_1)
        face_z(l1, row, range(3), deep_1)
    for row in (1, 2, 3, 4, 5):
        face_x(l1, row, range(3))
    for row in (1, 6):
        face_y(l1, row, range(3), factors_1)
        face_z(l1, row, range(3), deep_1)
    for row in (3, 4):
        weigh(l1, row, range(3))
    mine = 4 + across
    coarse_fields(l2, l3, 1, 2, mine)
    arrive(fields_1)
    for row in (0, 6):
        face_x(l1, row, range(3))
    for row in (1, 2, 5, 6):
        weigh(l1, row, range(3))
    coarse_conduct(l1, l2, 1, 0, 1)
    coarse_conduct(l1, l2, 1, 6, 4)
    arrive(sources_1)
    smooth(l1, 1, 7, True)
    coarse_source(l1, l2, 2, 2, 2, True)

    sources_2 = [send(s2.at[pl.ds(3, 1)], s2.at[pl.ds(1, 1)], device(1)), send(s2.at[pl.ds(2, 1)], s2.at[pl.ds(4, 1)], device(-1))]
    smooths_1 = [send(l1.smooth.at[pl.ds(4, 1)], l1.smooth.at[pl.ds(0, 1)], device(1)), send(l1.smooth.at[pl.ds(3, 1)], l1.smooth.at[pl.ds(7, 1)], device(-1))]
    fields_3 = [
        send(db3.at[:, pl.ds(mine, 1)], db3.at[:, pl.ds(4 * (1 - dz) + across, 1)], ring_device(dz, dx)) for dz, dx in ring
    ]
    arrive(fields_2)
    faces(l2, 1, 5, True)
    arrive(sources_2)
    smooth(l2, 1, 5, True)
    coarse_source(l2, l3, 1, 2, mine, True)

    sources_3 = [
        send(s3.at[pl.ds(mine, 1)], s3.at[pl.ds(4 * (1 - dz) + across, 1)], ring_device(dz, dx)) for dz, dx in ring
    ]
    smooths_2 = [send(l2.smooth.at[pl.ds(2, 1)], l2.smooth.at[pl.ds(0, 1)], device(1)), send(l2.smooth.at[pl.ds(3, 1)], l2.smooth.at[pl.ds(5, 1)], device(-1))]
    arrive(fields_3)
    coarse_fields(l3, l4, 6, 0, 0)
    coarse_fields(l4, l5, 1, 2, 4)
    for i in range(2):
        packed_fields[i, 4] = pack(db5[i, 4])
    fields_5 = [
        send(packed_fields.at[:, pl.ds(4, 1)], packed_fields.at[:, pl.ds(4 - dz, 1)], device(4 * dz)) for dz in (4, -4, 3, -3, 2, -2, 1, -1)
    ]
    faces(l3, 1, 11, False)
    faces(l4, 1, 5, True)
    arrive(sources_3)
    smooth(l3, 1, 11, True)
    coarse_source(l3, l4, 4, 2, 1, True)
    smooth(l4, 1, 5, True)
    coarse_source(l4, l5, 1, 2, 4, True)

    packed_source[4] = pack(s5[4])
    sources_5 = [send(packed_source.at[pl.ds(4, 1)], packed_source.at[pl.ds(4 - dz, 1)], device(4 * dz)) for dz in (3, -3, 2, -2, 1, -1)]
    smooths_4 = [send(l4.smooth.at[pl.ds(2, 1)], l4.smooth.at[pl.ds(0, 1)], device(4)), send(l4.smooth.at[pl.ds(3, 1)], l4.smooth.at[pl.ds(5, 1)], device(-4))]
    arrive(fields_5)
    for row in (0, 1, 2, 3, 5, 6, 7, 8):
        for i in range(2):
            db5[i, row] = unpack(packed_fields[i, row])
    faces(l5, 1, 8, True)
    arrive(sources_5)
    for row in (1, 2, 3, 5, 6, 7):
        s5[row] = unpack(packed_source[row])

    smooth(l5, 1, 8, True)

    def into(ref):
        return lambda row, tile, value: put(ref, row, tile, value)

    relax(l5, l5.smooth, 2, 7, into(l5.work), True)
    relax(l5, l5.work, 3, 6, into(iterates[5]), True)

    def lift(fine, coarse_ref, coarse_rows, coarse_tiles, first_row, last_row, coarse_of):
        values = [jnp.concatenate([tile_of(coarse_ref, c, t) for c in coarse_rows], axis=0) for t in range(coarse_tiles)]
        for t in range(fine.tiles):
            spread_out = exact_dot(values[t // 2], spread[t % 2])
            for row in range(first_row, last_row):
                at = coarse_of(row)
                put(lifts, row, t, tile_of(fine.smooth, row, t) + spread_out[at * NZ : (at + 1) * NZ])

    arrive(smooths_4)
    lift(l4, iterates[5], range(3, 6), 1, 0, 6, lambda row: row // 2)
    relax(l4, lifts, 1, 5, into(iterates[4]), True)
    lift(l3, iterates[4], range(1, 5), 1, 2, 10, lambda row: row // 2 - 1)
    relax(l3, lifts, 3, 9, into(iterates[3]), True)
    arrive(smooths_2)
    lift(l2, iterates[3], [across + 3 + i for i in range(3)], 1, 0, 6, lambda row: row // 2)
    relax(l2, lifts, 1, 5, into(iterates[2]), True)
    arrive(smooths_1)
    lift(l1, iterates[2], range(1, 5), 2, 0, 8, lambda row: row // 2)
    relax(l1, lifts, 1, 7, into(iterates[1]), True)
    lift(l0, iterates[1], range(1, 7), 3, 1, 11, lambda row: (row - 2) // 2 + 1)

    stores = []

    def finish(row, tile, value):
        put(staged, row - 2, tile - 1, value)
        if tile == 4:
            stores.append(pltpu.make_async_copy(staged.at[row - 2], out_ref.at[:, row - 2, :], local_sem.at[row - 2]))
            stores[-1].start()

    relax(l0, lifts, 2, 10, finish, True, range(1, 5))
    for copy in stores:
        copy.wait()
    for copy in copies:
        copy.wait_send()


def shapes():
    def rows(level, *lead):
        return pltpu.VMEM((*lead, ROWS[level], NZ, TILES[level] * LANES), F32)

    first = [rows(0), rows(0, 2), rows(1, 2), rows(1), rows(2, 2), rows(2), rows(3, 2), rows(3), rows(5, 2), rows(5)]
    first += [rows(4), rows(4), rows(4)]
    for level in range(6):
        first += [rows(level) for _ in range(6)]
    first += [pltpu.VMEM((4, NZ, TILES[0] * LANES), F32), pltpu.VMEM((12, NZ, TILES[0] * LANES), F32)]
    first += [rows(level) for level in range(6)]
    first += [pltpu.VMEM((8, NZ, 512), F32), pltpu.VMEM((2, 9, 8, LANES), F32), pltpu.VMEM((9, 8, LANES), F32), pltpu.SemaphoreType.DMA((24,))]
    return first + [pltpu.SemaphoreType.DMA((N_SEMS,)), pltpu.SemaphoreType.DMA((N_SEMS,))]


def on_device(right_side, diffusivity, reaction):
    return pl.pallas_call(
        kernel,
        out_shape=jax.ShapeDtypeStruct((NZ, 8, 512), F32),
        in_specs=[pl.BlockSpec(memory_space=pl.ANY)] * 3,
        out_specs=pl.BlockSpec(memory_space=pl.ANY),
        scratch_shapes=shapes(),
        compiler_params=pltpu.CompilerParams(collective_id=0, has_side_effects=True, vmem_limit_bytes=VMEM_BYTES),
    )(right_side, diffusivity, reaction)


def solution(mesh):
    specs = P(None, "span", "width")
    return jax.shard_map(on_device, mesh=mesh, in_specs=(specs,) * 3, out_specs=specs, check_vma=False)
```
